256 devices in a mesh: section: 2 (over core), dp: 32 (over z, x), mp: 4 (over y).
Axes of the slice: x: 4, y: 4, z: 8, core: 2. Of those that a mesh axis runs over, the one named last changes fastest.
Arguments:
- features: bfloat16 [32768, 4096], P(('section', 'dp'), 'mp'), may hold values from -16 to 16
- w_in: bfloat16 [4096, 2048], P(('section', 'dp'), 'mp'), may hold values from -0.09375 to 0.09375
- w_out: bfloat16 [512, 2048], P(('section', 'dp'), 'mp'), may hold values from -0.125 to 0.125
- codebook: bfloat16 [3, 65536, 512], P(None, ('section', 'dp'), 'mp'), may hold values from -3 to 3
- codes: int32 [3, 32768], P(None, ('section', 'dp')), may hold values from 0 to 65535, as said below
- decoder_grad: bfloat16 [32768, 512], P(('section', 'dp'), 'mp'), may hold values from -16 to 16
Outputs:
- in_grad: float32 [4096, 2048], P(('section', 'dp'), 'mp')
- out_grad: float32 [512, 2048], P(('section', 'dp'), 'mp')
- code_sums: float32 [3, 65536, 512], P(None, ('section', 'dp'), 'mp')
The draws below stay inside these ranges and needn't reach their ends.
Inputs may be any that keep to these rules, and one draw needn't show every extreme that they name: Row k of a level's codebook belongs to owner k // 1024. Within the 512 items of one device (aligned blocks of items), at each level at most 16 codes belong to one owner; at each level some owner receives exactly 16 codes from every device's items.
All inputs are finite; a program needn't handle non-finite values.
Results may differ from the reference program's by a relative error of at most 0.0026.
Values may be sent and summed in bfloat16 or wider, within the bound.
No kernel may reach another device: no remote copies, remote signals or barrier semaphores. Data moves between devices by JAX's collectives and lax.ppermute only.
A program may use at most 64 MiB of HBM per device.

```python
import jax
import jax.numpy as jnp
from jax import lax

D = 4096
H = 2048
L = 512
K = 65536
LEV = 3
ITEM_DEV = 512
OWNERS = 64
ITEMS = 32768
ROWS_OWN = 1024
CAP = 16


def draw_codes(key, part):
    levels = []
    for level_index in range(LEV):
        level_key = jax.random.fold_in(key, 17 + level_index)
        full_owner = jax.random.randint(jax.random.fold_in(level_key, 1), (), 0, OWNERS)
        block_keys = jax.random.split(jax.random.fold_in(level_key, 2), OWNERS)

        def one_block(block_key):
            pick_key, order_key, row_key = jax.random.split(block_key, 3)
            places = jax.random.permutation(pick_key, (OWNERS - 1) * CAP)[:ITEM_DEV - CAP]
            others = (places // CAP).astype(jnp.int32)
            others = others + (others >= full_owner).astype(jnp.int32)
            owners = jnp.concatenate([jnp.zeros((CAP,), jnp.int32) + full_owner, others])
            owners = jax.random.permutation(order_key, owners)
            offsets = jax.random.randint(row_key, (ITEM_DEV,), 0, ROWS_OWN)
            return owners * ROWS_OWN + offsets
        levels.append(jax.vmap(one_block)(block_keys).reshape(ITEMS))
    return jnp.stack(levels).astype(jnp.int32)


def strengthened(drawn, stream_key, source, target, blocks, factor):
    owner, partner = [(jnp.arange(drawn.shape[position]) // (drawn.shape[position] // blocks)).reshape([-1 if axis == position else 1 for axis in range(drawn.ndim)]) for position in (source, target)]
    chosen = jax.random.permutation(stream_key, blocks)[partner]
    strong = (owner == chosen) | (owner == (partner + blocks // 2) % blocks)
    return jnp.where(strong, factor * drawn, drawn)


def block_scale(own_key, shape, shards, smallest, largest):
    def one(axis_at, shards_of):
        draws = jax.random.uniform(jax.random.fold_in(jax.random.fold_in(own_key, 6), axis_at), (shards_of,), jnp.float32, smallest / len(shards), largest / len(shards))
        return jnp.repeat(jnp.exp(draws), shape[axis_at] // shards_of).reshape((-1,) + (1,) * (len(shape) - axis_at - 1))

    factor_of = one(*shards[0])
    for cut in shards[1:]:
        factor_of = factor_of * one(*cut)
    return factor_of


def centred(rng, extent, width, reach, cuts=(), held_as=jnp.bfloat16):
    result = width * jax.random.normal(rng, extent, jnp.float32)
    if cuts:
        result = result * block_scale(rng, extent, cuts, -0.22, 0.18)
    return jnp.clip(result, -reach, reach).astype(held_as)


def noise_with(rng, dims, spread, reach, cuts, heavy, kind=jnp.bfloat16):
    result = spread * jax.random.normal(rng, dims, jnp.float32)
    if cuts:
        result = result * block_scale(rng, dims, cuts, -0.22, 0.18)
    return jnp.clip(strengthened(result, jax.random.fold_in(rng, 3), *heavy), -reach, reach).astype(kind)


def setup_inputs(seed: int = 0) -> dict:
    keys = jax.random.split(jax.random.key(seed), 7)
    return {
        "features": noise_with(keys[0], (ITEMS, D), 1.0, 16.0, ((0, 64), (1, 4)), (0, 1, 64, 4.0)),
        "w_in": centred(keys[1], (D, H), D ** -0.5, 0.09375, ((0, 64), (1, 4))),
        "w_out": centred(keys[2], (L, H), H ** -0.5, 0.125, ((0, 64), (1, 4))),
        "codebook": centred(keys[3], (LEV, K, L), 0.5, 3.0, ((1, 64), (2, 4))),
        "codes": draw_codes(jax.random.fold_in(keys[6], 71), 0),
        "decoder_grad": noise_with(keys[5], (ITEMS, L), 1.0, 16.0, ((0, 64), (1, 4)), (0, 1, 64, 4.0)),
    }


BETA = 0.25

def silu_slope(preact):
    logistic = jax.nn.sigmoid(preact)
    return logistic * (1.0 + preact * (1.0 - logistic))

def reference(features, w_in, w_out, codebook, codes, decoder_grad):
    preact = jnp.dot(features, w_in, preferred_element_type=jnp.float32)
    hidden = jax.nn.silu(preact).astype(jnp.bfloat16)
    latent = lax.dot_general(hidden, w_out, (((1,), (1,)), ((), ())), preferred_element_type=jnp.float32)
    residual = latent
    pull_sum = jnp.zeros_like(latent)
    code_total = jnp.zeros((LEV * K, L), jnp.float32)
    for level_index in range(LEV):
        row_ids = codes[level_index].astype(jnp.int32)
        codeword = jnp.take(codebook[level_index], row_ids, axis=0).astype(jnp.float32)
        code_total = code_total.at[row_ids + level_index * K].add(residual)
        residual = residual - codeword
        pull_sum = pull_sum + residual
    latent_grad = ((decoder_grad.astype(jnp.float32) + 2.0 * BETA * pull_sum) / jnp.sqrt(jnp.float32(ITEMS))).astype(jnp.bfloat16)
    out_grad = lax.dot_general(latent_grad, hidden, (((0,), (0,)), ((), ())), preferred_element_type=jnp.float32)
    back_hidden = jnp.dot(latent_grad, w_out, preferred_element_type=jnp.float32)
    pre_grad = (back_hidden * silu_slope(preact)).astype(jnp.bfloat16)
    in_grad = lax.dot_general(features, pre_grad, (((0,), (0,)), ((), ())), preferred_element_type=jnp.float32)
    return (in_grad, out_grad, code_total.reshape(LEV, K, L))
```

```python
import jax
import jax.numpy as jnp
from jax import lax
from jax.sharding import Mesh, PartitionSpec as P

BETA = 0.25
BF = jnp.bfloat16
F32 = jnp.float32
OWN = ("s", "z", "x")


def shift(value, axis, by):
    size = lax.axis_size(axis)
    return lax.ppermute(value, axis, [(i, (i + by) % size) for i in range(size)])


def mm(a, b, dims=((1,), (0,))):
    return lax.dot_general(a, b, (dims, ((), ())), preferred_element_type=F32)


def exchange(value, axis):
    return lax.all_to_all(value, axis, split_axis=0, concat_axis=0, tiled=True)


def spread(value, axis):
    size = lax.axis_size(axis)
    return exchange(jnp.broadcast_to(value[None], (size,) + value.shape), axis)


def shards(features, w_in, w_out, codebook, codes, decoder_grad):
    s, y = lax.axis_index("s"), lax.axis_index("y")
    ns, nz, nx, ny = (lax.axis_size(a) for a in ("s", "z", "x", "y"))
    owners = ns * nz * nx
    items, depth = features.shape
    levels, rows_own, width = codebook.shape
    cap = 2 * items // owners
    slots = owners * cap
    hid = w_in.shape[1]
    in_rows, out_rows = w_in.shape[0], w_out.shape[0]
    both = in_rows + out_rows
    items_all = items * owners
    half = items // 2

    top, bot = features[:half], features[half:]
    left_top = shift(top, "y", 1)
    right_bot = shift(bot, "y", -1)
    left_bot = shift(bot, "y", 1)
    right_top = shift(top, "y", -1)
    far_top = shift(left_top, "y", 1)
    far_bot = shift(right_bot, "y", -1)

    w_mine = jnp.concatenate([w_in, w_out], axis=0)
    w_z = spread(w_mine, "z")
    w_x = spread(w_z, "x")
    w_half = jnp.transpose(w_x, (1, 0, 2, 3))
    w_in_half = w_half[:, :, :in_rows].reshape(nz * nx * in_rows, hid)
    w_out_half = w_half[:, :, in_rows:].reshape(nz * nx * out_rows, hid)
    w_in_other = shift(w_in_half, "s", 1)
    w_out_other = shift(w_out_half, "s", 1)
    w_in_part = jnp.stack([w_in_half, w_in_other]).reshape(ny, depth, hid)
    w_out_part = jnp.stack([w_out_half, w_out_other]).reshape(ny, width, hid)

    def place(k):
        return (y - k - (ny // ns) * s) % ny

    parts = [(0, top, bot), (1, left_top, left_bot), (3, right_top, right_bot), (2, far_top, far_bot)]
    feats = jnp.zeros((ny, items, depth), BF)
    for k, a, b in parts:
        feats = lax.dynamic_update_slice(feats, a[None], (place(k), 0, 0))
        feats = lax.dynamic_update_slice(feats, b[None], (place(k), half, 0))

    owner_of = codes // rows_own
    row_of = codes % rows_own
    item_ids = jnp.arange(items)
    lower = (item_ids[None, :] <= item_ids[:, None]).astype(BF)
    slot_ids = jnp.arange(slots)
    slot_list, asked_in = [], []
    for l in range(levels):
        match = (owner_of[l][:, None] == jnp.arange(owners)[None, :]).astype(BF)
        upto = mm(lower, match)
        rank = jnp.sum(upto * match.astype(F32), axis=1).astype(jnp.int32) - 1
        slot = owner_of[l] * cap + rank
        slot_list.append(slot)
        marks = jnp.stack([row_of[l] // 32, row_of[l] % 32, jnp.ones_like(row_of[l])]).astype(BF)
        put = mm(marks, (slot[:, None] == slot_ids[None, :]).astype(BF))
        want = jnp.where(put[2] > 0, put[0] * 32 + put[1], -1.0).astype(jnp.int32)
        asked_in.append(want.reshape(owners, cap))
    asked = exchange(jnp.concatenate(asked_in, axis=1), OWN)
    asked_list = [asked[:, l * cap:(l + 1) * cap].reshape(slots) for l in range(levels)]
    row_ids = jnp.arange(rows_own)
    rows_out = [
        mm((asked_list[l][:, None] == row_ids[None, :]).astype(BF), codebook[l]).astype(BF).reshape(owners, cap, width)
        for l in range(levels)
    ]
    rows_back = exchange(jnp.concatenate(rows_out, axis=1), OWN)
    words = [
        mm(
            (slot_list[l][:, None] == slot_ids[None, :]).astype(BF),
            rows_back[:, l * cap:(l + 1) * cap].reshape(slots, width),
        )
        for l in range(levels)
    ]

    preact = mm(feats[0], w_in_part[0])
    for p in range(1, ny):
        preact = preact + mm(feats[p], w_in_part[p])
    logistic = jax.nn.sigmoid(preact)
    hidden = (preact * logistic).astype(BF)
    slope = logistic * (1.0 + preact * (1.0 - logistic))

    def w_out_at(q):
        return lax.dynamic_index_in_dim(w_out_part, (q - (ny // ns) * s) % ny, 0, keepdims=False)

    far = shift(mm(hidden, w_out_at(y + 2), ((1,), (1,))), "y", 2)
    fwd = shift(mm(hidden, w_out_at(y + 1), ((1,), (1,))), "y", 1)
    bwd = shift(mm(hidden, w_out_at(y - 1), ((1,), (1,))), "y", -1)
    latent = mm(hidden, w_out_at(y), ((1,), (1,))) + fwd + bwd + far

    residual = latent
    pull_sum = jnp.zeros_like(latent)
    outgoing = []
    for l in range(levels):
        placed = mm((slot_ids[:, None] == slot_list[l][None, :]).astype(BF), residual.astype(BF))
        outgoing.append(placed.astype(BF).reshape(owners, cap, width))
        residual = residual - words[l]
        pull_sum = pull_sum + residual
    latent_grad = (
        (decoder_grad.astype(F32) + 2.0 * BETA * pull_sum) / jnp.sqrt(F32(items_all))
    ).astype(BF)
    grads = [latent_grad, shift(latent_grad, "y", 1), shift(latent_grad, "y", 2), shift(latent_grad, "y", -1)]
    grad_rel = jnp.concatenate(grads, axis=1)
    w_out_rel = jnp.concatenate([w_out_at(y - k) for k in range(ny)], axis=0)
    pre_grad = (mm(grad_rel, w_out_rel) * slope).astype(BF)

    incoming = exchange(jnp.concatenate(outgoing, axis=1), OWN)
    code_sums = jnp.stack([
        mm(
            (row_ids[:, None] == asked_list[l][None, :]).astype(BF),
            incoming[:, l * cap:(l + 1) * cap].reshape(slots, width),
        )
        for l in range(levels)
    ])

    out_rel = mm(grad_rel, hidden, ((0,), (0,))).reshape(ny, width, hid)
    out_at = lambda p: lax.dynamic_index_in_dim(out_rel, (y - p - (ny // ns) * s) % ny, 0, keepdims=False)
    hy = ny // ns
    out_other = shift(jnp.stack([out_at(p) for p in range(hy, ny)]), "s", 1)
    out_sum = (jnp.stack([out_at(p) for p in range(hy)]) + out_other).reshape(nz, nx, out_rows, hid)
    pieces = 2
    step = hid // pieces
    in_list, out_list = [], []
    for c in range(pieces):
        cut = pre_grad[:, c * step:(c + 1) * step]
        there = jnp.stack([mm(feats[p], cut, ((0,), (0,))) for p in range(hy, ny)])
        came = shift(there, "s", 1)
        here = jnp.stack([mm(feats[p], cut, ((0,), (0,))) for p in range(hy)])
        in_sum = (here + came).reshape(nz, nx, in_rows, step)
        pair = jnp.concatenate([in_sum, out_sum[..., c * step:(c + 1) * step]], axis=2)
        over_x = exchange(jnp.transpose(pair, (1, 0, 2, 3)).astype(BF), "x")
        sum_x = jnp.sum(over_x.astype(F32), axis=0)
        over_z = exchange(sum_x.astype(BF), "z")
        sum_z = jnp.sum(over_z.astype(F32), axis=0)
        in_list.append(sum_z[:in_rows])
        out_list.append(sum_z[in_rows:])
    return (jnp.concatenate(in_list, axis=1), jnp.concatenate(out_list, axis=1), code_sums)


def solution(mesh):
    fine = Mesh(mesh.devices.reshape(2, 8, 4, 4), ("s", "z", "x", "y"))
    in_specs = (
        P(OWN, "y"),
        P(OWN, "y"),
        P(OWN, "y"),
        P(None, OWN, "y"),
        P(None, OWN),
        P(OWN, "y"),
    )
    out_specs = (P(OWN, "y"), P(OWN, "y"), P(None, OWN, "y"))
    return jax.shard_map(shards, mesh=fine, in_specs=in_specs, out_specs=out_specs, check_vma=False)
```

```python
import jax
import jax.numpy as jnp
from jax import lax
from jax.sharding import Mesh, PartitionSpec as P

BETA = 0.25
BF = jnp.bfloat16
F32 = jnp.float32
OWN = ("s", "z", "x")


def shift(value, axis, by):
    size = lax.axis_size(axis)
    return lax.ppermute(value, axis, [(i, (i + by) % size) for i in range(size)])


def mm(a, b, dims=((1,), (0,))):
    return lax.dot_general(a, b, (dims, ((), ())), preferred_element_type=F32)


def exchange(value, axis):
    return lax.all_to_all(value, axis, split_axis=0, concat_axis=0, tiled=True)


def at(stacked, index):
    return lax.dynamic_index_in_dim(stacked, index, 0, keepdims=False)


def put(stacked, value, *index):
    value = value.reshape((1,) * (stacked.ndim - value.ndim) + value.shape)
    index = tuple(index) + (0,) * (stacked.ndim - len(index))
    return lax.dynamic_update_slice(stacked, value, index)


def shards(features, w_in, w_out, codebook, codes, decoder_grad):
    s, x, y = lax.axis_index("s"), lax.axis_index("x"), lax.axis_index("y")
    ns, nz, nx, ny = (lax.axis_size(a) for a in ("s", "z", "x", "y"))
    owners = ns * nz * nx
    items, depth = features.shape
    levels, rows_own, width = codebook.shape
    cap = 2 * items // owners
    slots = owners * cap
    hid = w_in.shape[1]
    in_rows, out_rows = w_in.shape[0], w_out.shape[0]
    items_all = items * owners
    half = items // 2
    hy = ny // ns

    w_mine = jnp.concatenate([w_in, w_out], axis=0)
    w_z = exchange(jnp.broadcast_to(w_mine[None], (nz,) + w_mine.shape), "z")

    top, bot = features[:half], features[half:]
    left_top = shift(top, "y", 1)
    right_bot = shift(bot, "y", -1)
    left_bot = shift(bot, "y", 1)
    right_top = shift(top, "y", -1)
    far_top = shift(left_top, "y", 1)
    far_bot = shift(right_bot, "y", -1)

    blocks = [(0, w_z), (1, shift(w_z, "x", 1)), (3, shift(w_z, "x", -1)), (2, shift(w_z, "x", 2))]
    w_in_part = jnp.zeros((ns, nz, nx, in_rows, hid), BF)
    w_out_part = jnp.zeros((ns, nz, nx, out_rows, hid), BF)
    for k, block in blocks:
        other = shift(block, "s", 1)
        for r, got in enumerate((block, other)):
            got = got[:, None]
            w_in_part = put(w_in_part, got[:, :, :in_rows], r, 0, (x - k) % nx)
            w_out_part = put(w_out_part, got[:, :, in_rows:], r, 0, (x - k) % nx)
    w_in_part = w_in_part.reshape(ny, depth, hid)
    w_out_part = w_out_part.reshape(ny, width, hid)

    parts = [(0, top, bot), (1, left_top, left_bot), (3, right_top, right_bot), (2, far_top, far_bot)]
    feats = jnp.zeros((ny, items, depth), BF)
    feats_t = jnp.zeros((ny, depth, items), BF)
    for k, first, second in parts:
        place = (y - k - hy * s) % ny
        feats = put(feats, first, place)
        feats = put(feats, second, place, half)
        feats_t = put(feats_t, first.T, place)
        feats_t = put(feats_t, second.T, place, 0, half)

    owner_of = codes // rows_own
    row_of = codes % rows_own
    item_ids = jnp.arange(items)
    lower = (item_ids[None, :] <= item_ids[:, None]).astype(BF)
    slot_ids = jnp.arange(slots)
    slot_list, asked_in = [], []
    for l in range(levels):
        match = (owner_of[l][:, None] == jnp.arange(owners)[None, :]).astype(BF)
        upto = mm(lower, match)
        rank = jnp.sum(upto * match.astype(F32), axis=1).astype(jnp.int32) - 1
        slot = owner_of[l] * cap + rank
        slot_list.append(slot)
        marks = jnp.stack([row_of[l] // 32, row_of[l] % 32, jnp.ones_like(row_of[l])]).astype(BF)
        found = mm(marks, (slot[:, None] == slot_ids[None, :]).astype(BF))
        want = jnp.where(found[2] > 0, found[0] * 32 + found[1], -1.0).astype(jnp.int32)
        asked_in.append(want.reshape(owners, cap))
    asked = exchange(jnp.concatenate(asked_in, axis=1), OWN)
    asked_list = [asked[:, l * cap:(l + 1) * cap].reshape(slots) for l in range(levels)]
    row_ids = jnp.arange(rows_own)
    rows_out = [
        mm((asked_list[l][:, None] == row_ids[None, :]).astype(BF), codebook[l]).astype(BF).reshape(owners, cap, width)
        for l in range(levels)
    ]
    rows_back = exchange(jnp.concatenate(rows_out, axis=1), OWN)
    words = [
        mm(
            (slot_list[l][:, None] == slot_ids[None, :]).astype(BF),
            rows_back[:, l * cap:(l + 1) * cap].reshape(slots, width),
        )
        for l in range(levels)
    ]

    preact = mm(feats[0], w_in_part[0])
    for p in range(1, ny):
        preact = preact + mm(feats[p], w_in_part[p])
    logistic = jax.nn.sigmoid(preact)
    hidden = (preact * logistic).astype(BF)
    slope = logistic * (1.0 + preact * (1.0 - logistic))

    def w_out_at(q):
        return at(w_out_part, (q - hy * s) % ny)

    far = shift(mm(hidden, w_out_at(y + 2), ((1,), (1,))), "y", 2)
    fwd = shift(mm(hidden, w_out_at(y + 1), ((1,), (1,))), "y", 1)
    bwd = shift(mm(hidden, w_out_at(y - 1), ((1,), (1,))), "y", -1)
    words = lax.optimization_barrier(words)
    latent = mm(hidden, w_out_at(y), ((1,), (1,))) + fwd + bwd + far

    residual = latent
    pull_sum = jnp.zeros_like(latent)
    outgoing = []
    for l in range(levels):
        placed = mm((slot_ids[:, None] == slot_list[l][None, :]).astype(BF), residual.astype(BF))
        outgoing.append(placed.astype(BF).reshape(owners, cap, width))
        residual = residual - words[l]
        pull_sum = pull_sum + residual
    latent_grad = (
        (decoder_grad.astype(F32) + 2.0 * BETA * pull_sum) / jnp.sqrt(F32(items_all))
    ).astype(BF)
    grads = [
        latent_grad,
        shift(latent_grad, "y", 1),
        shift(latent_grad, "y", 2),
        shift(latent_grad, "y", -1),
    ]
    grad_rel = jnp.concatenate(grads, axis=1)
    w_out_rel = jnp.concatenate([w_out_at(y - k) for k in range(ny)], axis=0)
    pre_grad = (mm(grad_rel, w_out_rel) * slope).astype(BF)

    incoming = exchange(jnp.concatenate(outgoing, axis=1), OWN)
    code_sums = jnp.stack([
        mm(
            (row_ids[:, None] == asked_list[l][None, :]).astype(BF),
            incoming[:, l * cap:(l + 1) * cap].reshape(slots, width),
        )
        for l in range(levels)
    ])

    out_rel = mm(grad_rel, hidden, ((0,), (0,))).reshape(ny, width, hid)
    out_at = lambda p: at(out_rel, (y - p - hy * s) % ny)
    out_other = shift(jnp.stack([out_at(p) for p in range(hy, ny)]), "s", 1)
    out_sum = (jnp.stack([out_at(p) for p in range(hy)]) + out_other).reshape(nz, nx, out_rows, hid)
    pieces = 2
    step = hid // pieces
    in_list, out_list = [], []
    for c in range(pieces):
        cut = pre_grad[:, c * step:(c + 1) * step]
        there = jnp.stack([mm(feats_t[p], cut) for p in range(hy, ny)])
        came = shift(there, "s", 1)
        here = jnp.stack([mm(feats_t[p], cut) for p in range(hy)])
        in_sum = (here + came).reshape(nz, nx, in_rows, step)
        pair = jnp.concatenate([in_sum, out_sum[..., c * step:(c + 1) * step]], axis=2)
        of = lambda q: lax.dynamic_index_in_dim(pair, q % nx, 1, keepdims=False)
        sum_x = (
            of(x)
            + shift(of(x + 1).astype(BF), "x", 1).astype(F32)
            + shift(of(x - 1).astype(BF), "x", -1).astype(F32)
            + shift(of(x + 2).astype(BF), "x", 2).astype(F32)
        )
        over_z = exchange(sum_x.astype(BF), "z")
        sum_z = jnp.sum(over_z.astype(F32), axis=0)
        in_list.append(sum_z[:in_rows])
        out_list.append(sum_z[in_rows:])
    return (jnp.concatenate(in_list, axis=1), jnp.concatenate(out_list, axis=1), code_sums)


def solution(mesh):
    fine = Mesh(mesh.devices.reshape(2, 8, 4, 4), ("s", "z", "x", "y"))
    in_specs = (
        P(OWN, "y"),
        P(OWN, "y"),
        P(OWN, "y"),
        P(None, OWN, "y"),
        P(None, OWN),
        P(OWN, "y"),
    )
    out_specs = (P(OWN, "y"), P(OWN, "y"), P(None, OWN, "y"))
    return jax.shard_map(shards, mesh=fine, in_specs=in_specs, out_specs=out_specs, check_vma=False)
```

```python
import jax
import jax.numpy as jnp
from jax import lax
from jax.experimental import pallas as pl
from jax.experimental.pallas import tpu as pltpu
from jax.sharding import Mesh, PartitionSpec as P

BETA = 0.25
BF = jnp.bfloat16
F32 = jnp.float32
I32 = jnp.int32
OWN = ("s", "z", "x")
VMEM = pl.BlockSpec(memory_space=pltpu.VMEM)
SMEM = pl.BlockSpec(memory_space=pltpu.SMEM)


def shift(value, axis, by):
    size = lax.axis_size(axis)
    return lax.ppermute(value, axis, [(i, (i + by) % size) for i in range(size)])


def exchange(value, axis):
    return lax.all_to_all(value, axis, split_axis=0, concat_axis=0, tiled=True)


def mm(a, b, dims=((1,), (0,))):
    return lax.dot_general(a, b, (dims, ((), ())), preferred_element_type=F32)


def encode(feats, near, other, place, in_rows):
    items, depth = feats[0].shape
    nz, both, hid = near[0].shape
    nx = len(near)
    out_rows = both - in_rows
    ny = len(feats)
    hz = nz * 2 // ny
    width = hz * nx * out_rows
    tile = items // 2

    def kernel(place_ref, *refs):
        f_refs, refs = refs[:ny], refs[ny:]
        n_refs, refs = refs[:nx], refs[nx:]
        o_refs, refs = refs[:nx], refs[nx:]
        hid_ref, slope_ref, wo_ref = refs[:3]
        lat_refs, (w_ref, wo32_ref) = refs[3:3 + ny], refs[3 + ny:]
        for k in range(nx):
            xk = place_ref[k]
            for r, ref in enumerate((n_refs[k], o_refs[k])):
                for zh in range(ny // 2):
                    p = r * (ny // 2) + zh
                    cut = ref[zh * hz:(zh + 1) * hz]
                    w_ref[p, :, xk] = cut[:, :in_rows]
                    wo32_ref[p, :, xk] = cut[:, in_rows:].astype(F32)
        for p in range(ny):
            wo_ref[p] = wo32_ref[p].reshape(width, hid).astype(BF)

        def step(t, carry):
            rows = pl.ds(t * tile, tile)
            acc = None
            for k in range(ny):
                part = mm(f_refs[k][rows, :], w_ref[place_ref[nx + k]].reshape(depth, hid))
                acc = part if acc is None else acc + part
            logistic = jax.nn.sigmoid(acc)
            hidden = (acc * logistic).astype(BF)
            hid_ref[rows, :] = hidden
            slope_ref[rows, :] = logistic * (1.0 + acc * (1.0 - logistic))
            for j in range(ny):
                lat_refs[j][rows, :] = mm(hidden, wo_ref[place_ref[nx + ny + j]], ((1,), (1,)))
            return carry

        lax.fori_loop(0, items // tile, step, 0)

    return pl.pallas_call(
        kernel,
        out_shape=[
            jax.ShapeDtypeStruct((items, hid), BF),
            jax.ShapeDtypeStruct((items, hid), F32),
            jax.ShapeDtypeStruct((ny, width, hid), BF),
        ] + [jax.ShapeDtypeStruct((items, width), F32)] * ny,
        in_specs=[SMEM] + [VMEM] * (ny + 2 * nx),
        out_specs=[VMEM] * (3 + ny),
        scratch_shapes=[
            pltpu.VMEM((ny, hz, nx, in_rows, hid), BF),
            pltpu.VMEM((ny, hz, nx, out_rows, hid), F32),
        ],
        compiler_params=pltpu.CompilerParams(vmem_limit_bytes=48 * 1024 * 1024),
        cost_estimate=pl.CostEstimate(
            flops=2 * items * hid * ny * (depth + width), bytes_accessed=12 << 20, transcendentals=items * hid),
        name="encode",
    )(place, *feats, *near, *other)


def turn(feats, place):
    items, depth = feats[0].shape
    ny = len(feats)
    cols = 256

    def kernel(place_ref, *refs):
        for k in range(ny):
            refs[ny][place_ref[k]] = refs[k][...].T

    return pl.pallas_call(
        kernel,
        out_shape=jax.ShapeDtypeStruct((ny, depth, items), BF),
        grid=(depth // cols,),
        in_specs=[SMEM] + [pl.BlockSpec((items, cols), lambda i: (0, i))] * ny,
        out_specs=pl.BlockSpec((ny, cols, items), lambda i: (0, i, 0)),
        cost_estimate=pl.CostEstimate(flops=0, bytes_accessed=8 << 20, transcendentals=0),
        name="turn",
    )(place, *feats)


def back(grads, hidden, slope, w_out, place):
    items, hid = hidden.shape
    ny, width = w_out.shape[:2]

    def kernel(place_ref, *refs):
        g_refs, (hid_ref, slope_ref, wo_ref, pre_ref, out_ref) = refs[:ny], refs[ny:]
        acc = None
        for k in range(ny):
            part = mm(g_refs[k][...], wo_ref[place_ref[k]])
            acc = part if acc is None else acc + part
            out_ref[place_ref[k]] = mm(g_refs[k][...], hid_ref[...], ((0,), (0,)))
        pre_ref[...] = (acc * slope_ref[...]).astype(BF)

    return pl.pallas_call(
        kernel,
        out_shape=[
            jax.ShapeDtypeStruct((items, hid), BF),
            jax.ShapeDtypeStruct((ny, width, hid), F32),
        ],
        in_specs=[SMEM] + [VMEM] * (ny + 3),
        out_specs=[VMEM] * 2,
        cost_estimate=pl.CostEstimate(flops=4 * items * hid * ny * width, bytes_accessed=4 << 20, transcendentals=0),
        name="back",
    )(place, *grads, hidden, slope, w_out)


def cut_by_x(feats_t, pre, came, out_mine, out_came, order, nz, nx, c):
    ny, depth, items = feats_t.shape
    hid = came.shape[1]
    in_rows = came.shape[0] // (nz * nx)
    width = out_mine.shape[1]
    out_rows = ny * width // (2 * nz * nx)
    both = in_rows + out_rows
    feats_t = feats_t.reshape(ny * depth, items)
    out_mine = out_mine.reshape(ny * width, -1)
    out_came = out_came.reshape(ny * width, -1)

    def kernel(order_ref, f_ref, p_ref, came_ref, om_ref, oc_ref, own_ref, *rest):
        sends, part = rest[:-1], rest[-1]
        total = mm(f_ref[...], p_ref[...]) + came_ref[...]
        part[:, :in_rows] = total.reshape(nx, in_rows, hid)
        part[:, in_rows:] = (om_ref[...] + oc_ref[...]).reshape(nx, out_rows, hid)
        own_ref[0] = part[order_ref[0]]
        for k, send in enumerate(sends):
            send[0] = part[order_ref[k + 1]].astype(BF)

    block = pl.BlockSpec((1, both, hid), lambda z: (z, 0, 0))
    return pl.pallas_call(
        kernel,
        out_shape=[jax.ShapeDtypeStruct((nz, both, hid), F32)]
        + [jax.ShapeDtypeStruct((nz, both, hid), BF)] * (nx - 1),
        grid=(nz,),
        in_specs=[
            SMEM,
            pl.BlockSpec((nx * in_rows, items), lambda z: (z, 0)),
            pl.BlockSpec((items, hid), lambda z: (0, c)),
            pl.BlockSpec((nx * in_rows, hid), lambda z: (z, 0)),
            pl.BlockSpec((nx * out_rows, hid), lambda z: (z, c)),
            pl.BlockSpec((nx * out_rows, hid), lambda z: (nz + z, c)),
        ],
        out_specs=[block] * nx,
        scratch_shapes=[pltpu.VMEM((nx, both, hid), F32)],
        cost_estimate=pl.CostEstimate(
            flops=2 * nz * nx * in_rows * items * hid, bytes_accessed=8 << 20, transcendentals=0),
        name="cut_by_x",
    )(order, feats_t, pre, came, out_mine, out_came)


def shards(features, w_in, w_out, codebook, codes, decoder_grad):
    s, x, y = lax.axis_index("s"), lax.axis_index("x"), lax.axis_index("y")
    ns, nz, nx, ny = (lax.axis_size(a) for a in ("s", "z", "x", "y"))
    owners = ns * nz * nx
    items, depth = features.shape
    levels, rows_own, width = codebook.shape
    cap = 2 * items // owners
    slots = owners * cap
    hid = w_in.shape[1]
    in_rows = w_in.shape[0]
    items_all = items * owners
    hy = ny // ns

    w_mine = jnp.concatenate([w_in, w_out], axis=0)
    w_z = exchange(jnp.broadcast_to(w_mine[None], (nz,) + w_mine.shape), "z")
    feats = [features, shift(features, "y", 1), shift(features, "y", 2), shift(features, "y", -1)]
    near = [w_z, shift(w_z, "x", 1), shift(w_z, "x", 2), shift(w_z, "x", -1)]
    other = [shift(block, "s", 1) for block in near]
    steps = jnp.arange(ny, dtype=I32)
    x_place = (x - steps) % nx
    y_place = (y - steps - hy * s) % ny
    y_send = (y + steps - hy * s) % ny
    x_send = (x + steps) % nx

    owner_of = codes // rows_own
    row_of = codes % rows_own
    item_ids = jnp.arange(items)
    lower = (item_ids[None, :] <= item_ids[:, None]).astype(BF)
    slot_ids = jnp.arange(slots)
    slot_list, asked_in = [], []
    for l in range(levels):
        match = (owner_of[l][:, None] == jnp.arange(owners)[None, :]).astype(BF)
        upto = mm(lower, match)
        rank = jnp.sum(upto * match.astype(F32), axis=1).astype(jnp.int32) - 1
        slot = owner_of[l] * cap + rank
        slot_list.append(slot)
        marks = jnp.stack([row_of[l] // 32, row_of[l] % 32, jnp.ones_like(row_of[l])]).astype(BF)
        found = mm(marks, (slot[:, None] == slot_ids[None, :]).astype(BF))
        want = jnp.where(found[2] > 0, found[0] * 32 + found[1], -1.0).astype(jnp.int32)
        asked_in.append(want.reshape(owners, cap))
    asked = exchange(jnp.concatenate(asked_in, axis=1), OWN)
    asked_list = [asked[:, l * cap:(l + 1) * cap].reshape(slots) for l in range(levels)]
    row_ids = jnp.arange(rows_own)
    rows_out = [
        mm((asked_list[l][:, None] == row_ids[None, :]).astype(BF), codebook[l]).astype(BF).reshape(owners, cap, width)
        for l in range(levels)
    ]
    rows_back = exchange(jnp.concatenate(rows_out, axis=1), OWN)
    words = [
        mm(
            (slot_list[l][:, None] == slot_ids[None, :]).astype(BF),
            rows_back[:, l * cap:(l + 1) * cap].reshape(slots, width),
        )
        for l in range(levels)
    ]

    hidden, slope, w_out_all, *lat = encode(
        feats, near, other, jnp.concatenate([x_place, y_place, y_send]), in_rows
    )
    far = shift(lat[2], "y", 2)
    fwd = shift(lat[1], "y", 1)
    bwd = shift(lat[3], "y", -1)
    feats_t = turn(feats, y_place)
    words = lax.optimization_barrier(words)
    latent = lat[0] + fwd + bwd + far

    residual = latent
    pull_sum = jnp.zeros_like(latent)
    outgoing = []
    for l in range(levels):
        placed = mm((slot_ids[:, None] == slot_list[l][None, :]).astype(BF), residual.astype(BF))
        outgoing.append(placed.astype(BF).reshape(owners, cap, width))
        residual = residual - words[l]
        pull_sum = pull_sum + residual
    latent_grad = (
        (decoder_grad.astype(F32) + 2.0 * BETA * pull_sum) / jnp.sqrt(F32(items_all))
    ).astype(BF)
    grads = [
        latent_grad,
        shift(latent_grad, "y", 1),
        shift(latent_grad, "y", 2),
        shift(latent_grad, "y", -1),
    ]
    incoming = exchange(jnp.concatenate(outgoing, axis=1), OWN)
    code_sums = jnp.stack([
        mm(
            (row_ids[:, None] == asked_list[l][None, :]).astype(BF),
            incoming[:, l * cap:(l + 1) * cap].reshape(slots, width),
        )
        for l in range(levels)
    ])

    pre_grad, out_part = back(grads, hidden, slope, w_out_all, y_place)
    out_came = shift(out_part, "s", 1)
    pieces = 2
    step = hid // pieces
    there_rows = feats_t[hy:].reshape(hy * depth, items)
    sends = []
    for c in range(pieces):
        there = mm(there_rows, pre_grad[:, c * step:(c + 1) * step])
        came = shift(there, "s", 1)
        sends.append(cut_by_x(feats_t, pre_grad, came, out_part, out_came, x_send, nz, nx, c))
    in_list, out_list = [], []
    for c in range(pieces):
        own, to_1, to_2, to_3 = sends[c]
        sum_x = (
            own
            + shift(to_1, "x", 1).astype(F32)
            + shift(to_2, "x", 2).astype(F32)
            + shift(to_3, "x", -1).astype(F32)
        )
        over_z = exchange(sum_x.astype(BF), "z")
        sum_z = jnp.sum(over_z.astype(F32), axis=0)
        in_list.append(sum_z[:in_rows])
        out_list.append(sum_z[in_rows:])
    return (jnp.concatenate(in_list, axis=1), jnp.concatenate(out_list, axis=1), code_sums)


def solution(mesh):
    fine = Mesh(mesh.devices.reshape(2, 8, 4, 4), ("s", "z", "x", "y"))
    in_specs = (
        P(OWN, "y"),
        P(OWN, "y"),
        P(OWN, "y"),
        P(None, OWN, "y"),
        P(None, OWN),
        P(OWN, "y"),
    )
    out_specs = (P(OWN, "y"), P(OWN, "y"), P(None, OWN, "y"))
    return jax.shard_map(shards, mesh=fine, in_specs=in_specs, out_specs=out_specs, check_vma=False)
```

```python
import jax
import jax.numpy as jnp
from jax import lax
from jax.experimental import pallas as pl
from jax.experimental.pallas import tpu as pltpu
from jax.sharding import Mesh, PartitionSpec as P

BETA = 0.25
BF = jnp.bfloat16
F32 = jnp.float32
I32 = jnp.int32
OWN = ("s", "z", "x")
VMEM = pl.BlockSpec(memory_space=pltpu.VMEM)
SMEM = pl.BlockSpec(memory_space=pltpu.SMEM)


def shift(value, axis, by):
    size = lax.axis_size(axis)
    return lax.ppermute(value, axis, [(i, (i + by) % size) for i in range(size)])


def exchange(value, axis):
    return lax.all_to_all(value, axis, split_axis=0, concat_axis=0, tiled=True)


def mm(a, b, dims=((1,), (0,))):
    return lax.dot_general(a, b, (dims, ((), ())), preferred_element_type=F32)


def encode(feats, near, other, place, in_rows, out_rows):
    items, depth = feats[0].shape
    nz, _, hid = near[0].shape
    nx = len(near)
    ny = len(feats)
    hz = nz * 2 // ny
    width = hz * nx * out_rows
    tile = items // 2

    def kernel(place_ref, *refs):
        f_refs, refs = refs[:ny], refs[ny:]
        n_refs, refs = refs[:nx], refs[nx:]
        o_refs, refs = refs[:nx], refs[nx:]
        hid_ref, slope_ref, wo_ref = refs[:3]
        lat_refs, (w_ref, wo32_ref) = refs[3:3 + ny], refs[3 + ny:]
        for k in range(nx):
            xk = place_ref[k]
            for r, ref in enumerate((n_refs[k], o_refs[k])):
                for zh in range(ny // 2):
                    p = r * (ny // 2) + zh
                    cut = ref[zh * hz:(zh + 1) * hz]
                    w_ref[p, :, xk] = cut[:, :in_rows]
                    wo32_ref[p, :, xk] = cut[:, in_rows:].astype(F32)
        for p in range(ny):
            wo_ref[p] = wo32_ref[p].reshape(width, hid).astype(BF)

        def step(t, carry):
            rows = pl.ds(t * tile, tile)
            acc = None
            for k in range(ny):
                part = mm(f_refs[k][rows, :], w_ref[place_ref[nx + k]].reshape(depth, hid))
                acc = part if acc is None else acc + part
            logistic = jax.nn.sigmoid(acc)
            hidden = (acc * logistic).astype(BF)
            hid_ref[rows, :] = hidden
            slope_ref[rows, :] = logistic * (1.0 + acc * (1.0 - logistic))
            for j in range(ny):
                lat_refs[j][rows, :] = mm(hidden, wo_ref[place_ref[nx + ny + j]], ((1,), (1,)))
            return carry

        lax.fori_loop(0, items // tile, step, 0)

    return pl.pallas_call(
        kernel,
        out_shape=[
            jax.ShapeDtypeStruct((items, hid), BF),
            jax.ShapeDtypeStruct((items, hid), F32),
            jax.ShapeDtypeStruct((ny, width, hid), BF),
        ] + [jax.ShapeDtypeStruct((items, width), F32)] * ny,
        in_specs=[SMEM] + [VMEM] * (ny + 2 * nx),
        out_specs=[VMEM] * (3 + ny),
        scratch_shapes=[
            pltpu.VMEM((ny, hz, nx, in_rows, hid), BF),
            pltpu.VMEM((ny, hz, nx, out_rows, hid), F32),
        ],
        compiler_params=pltpu.CompilerParams(vmem_limit_bytes=48 * 1024 * 1024),
        cost_estimate=pl.CostEstimate(
            flops=2 * items * hid * ny * (depth + width), bytes_accessed=12 << 20, transcendentals=items * hid),
        name="encode",
    )(place, *feats, *near, *other)


def ask(codes, codes_t, w_in, w_out, nz, nx, ns, rows_own, cap):
    levels, items = codes.shape
    in_rows, hid = w_in.shape
    out_rows = w_out.shape[0]
    owners = ns * nz * nx
    slots = owners * cap
    group = slots // nz
    marks_rows = 8
    base = 32

    def owner_first(owner):
        section, rest = owner // (nz * nx), owner % (nz * nx)
        return (rest // nx * nx + rest % nx) * ns + section

    def kernel(codes_ref, codes_t_ref, wi_ref, wo_ref, slot_ref, pay_ref):
        first = lax.broadcasted_iota(I32, (items, items), 0)
        second = lax.broadcasted_iota(I32, (items, items), 1)
        lanes = lax.broadcasted_iota(I32, (items, slots), 1)
        line = lax.broadcasted_iota(I32, (marks_rows, items), 0)
        found = None
        for l in range(levels):
            code_row, code_col = codes_ref[l:l + 1, :], codes_t_ref[:, l:l + 1]
            own_row, own_col = code_row // rows_own, code_col // rows_own
            same = jnp.where(own_col == own_row, 1.0, 0.0)
            rank_row = jnp.sum(jnp.where(first < second, same, 0.0), axis=0, keepdims=True).astype(I32)
            rank_col = jnp.sum(jnp.where(second < first, same, 0.0), axis=1, keepdims=True).astype(I32)
            slot_ref[l:l + 1, :] = own_row * cap + rank_row
            spot = owner_first(own_col) * cap + rank_col
            value = code_row % rows_own + 1
            marks = jnp.where(line == 2 * l, value // base, jnp.where(line == 2 * l + 1, value % base, 0))
            hit = jnp.where(lanes == spot, 1.0, 0.0).astype(BF)
            part = mm(marks.astype(F32).astype(BF), hit)
            found = part if found is None else found + part
        rest = jnp.zeros((marks_rows, hid - group), F32)
        for z in range(nz):
            pay_ref[z, :in_rows] = wi_ref[...]
            digits = jnp.concatenate([found[:, z * group:(z + 1) * group], rest], axis=1)
            pay_ref[z, in_rows:] = jnp.concatenate([wo_ref[...].astype(F32), digits], axis=0).astype(BF)

    return pl.pallas_call(
        kernel,
        out_shape=[
            jax.ShapeDtypeStruct((levels, items), I32),
            jax.ShapeDtypeStruct((nz, in_rows + out_rows + marks_rows, hid), BF),
        ],
        in_specs=[VMEM] * 4,
        out_specs=[VMEM] * 2,
        name="ask",
    )(codes, codes_t, w_in, w_out)


def turn(feats, place):
    items, depth = feats[0].shape
    ny = len(feats)
    hy = ny // 2
    cols = 256

    def kernel(place_ref, *refs):
        here_ref, there_ref = refs[ny:]
        for k in range(ny):
            spot = place_ref[k]
            flat = refs[k][...].T

            @pl.when(spot < hy)
            def _():
                here_ref[spot] = flat

            @pl.when(spot >= hy)
            def _():
                there_ref[spot - hy] = flat

    out = pl.BlockSpec((hy, cols, items), lambda i: (0, i, 0))
    return pl.pallas_call(
        kernel,
        out_shape=[jax.ShapeDtypeStruct((hy, depth, items), BF)] * 2,
        grid=(depth // cols,),
        in_specs=[SMEM] + [pl.BlockSpec((items, cols), lambda i: (0, i))] * ny,
        out_specs=[out] * 2,
        cost_estimate=pl.CostEstimate(flops=0, bytes_accessed=8 << 20, transcendentals=0),
        name="turn",
    )(place, *feats)


def back(grads, hidden, slope, w_out, place):
    items, hid = hidden.shape
    ny, width = w_out.shape[:2]

    def kernel(place_ref, *refs):
        g_refs, (hid_ref, slope_ref, wo_ref, pre_ref, out_ref) = refs[:ny], refs[ny:]
        acc = None
        for k in range(ny):
            part = mm(g_refs[k][...], wo_ref[place_ref[k]])
            acc = part if acc is None else acc + part
            out_ref[place_ref[k]] = mm(g_refs[k][...], hid_ref[...], ((0,), (0,)))
        pre_ref[...] = (acc * slope_ref[...]).astype(BF)

    return pl.pallas_call(
        kernel,
        out_shape=[
            jax.ShapeDtypeStruct((items, hid), BF),
            jax.ShapeDtypeStruct((ny, width, hid), F32),
        ],
        in_specs=[SMEM] + [VMEM] * (ny + 3),
        out_specs=[VMEM] * 2,
        cost_estimate=pl.CostEstimate(flops=4 * items * hid * ny * width, bytes_accessed=4 << 20, transcendentals=0),
        name="back",
    )(place, *grads, hidden, slope, w_out)


def cut_by_x(feats_t, pre, came, out_mine, out_came, order, nz, nx, c):
    items = feats_t.shape[2]
    hid = came.shape[1]
    in_rows = came.shape[0] // (nz * nx)
    hy = feats_t.shape[0]
    ny, width = out_mine.shape[:2]
    out_rows = hy * width // (nz * nx)
    both = in_rows + out_rows
    feats_t = feats_t.reshape(-1, items)
    out_mine = out_mine.reshape(ny * width, -1)
    out_came = out_came.reshape(ny * width, -1)
    group = 2

    def kernel(order_ref, f_ref, p_ref, came_ref, om_ref, oc_ref, own_ref, *rest):
        sends, part = rest[:-1], rest[-1]
        pre_cut = p_ref[:, c * hid:(c + 1) * hid]

        def step(t, carry):
            many = group * nx * in_rows
            rows = pl.ds(pl.multiple_of(t * many, many), many)
            few = group * nx * out_rows
            mine = pl.ds(pl.multiple_of(t * few, few), few)
            far = pl.ds(pl.multiple_of(hy * width + t * few, few), few)
            total = (mm(f_ref[rows, :], pre_cut) + came_ref[rows, :]).reshape(group, nx, in_rows, hid)
            outs = om_ref[mine, c * hid:(c + 1) * hid] + oc_ref[far, c * hid:(c + 1) * hid]
            outs = outs.reshape(group, nx, out_rows, hid)
            for g in range(group):
                part[:, :in_rows] = total[g]
                part[:, in_rows:] = outs[g]
                own_ref[t * group + g] = part[order_ref[0]]
                for k, send in enumerate(sends):
                    send[t * group + g] = part[order_ref[k + 1]].astype(BF)
            return carry

        lax.fori_loop(0, nz // group, step, 0)

    return pl.pallas_call(
        kernel,
        out_shape=[jax.ShapeDtypeStruct((nz, both, hid), F32)]
        + [jax.ShapeDtypeStruct((nz, both, hid), BF)] * (nx - 1),
        in_specs=[SMEM] + [VMEM] * 5,
        out_specs=[VMEM] * nx,
        scratch_shapes=[pltpu.VMEM((nx, both, hid), F32)],
        cost_estimate=pl.CostEstimate(
            flops=2 * nz * nx * in_rows * items * hid, bytes_accessed=8 << 20, transcendentals=0),
        name="cut_by_x",
    )(order, feats_t, pre, came, out_mine, out_came)


def shards(features, w_in, w_out, codebook, codes, decoder_grad):
    s, x, y = lax.axis_index("s"), lax.axis_index("x"), lax.axis_index("y")
    ns, nz, nx, ny = (lax.axis_size(a) for a in ("s", "z", "x", "y"))
    owners = ns * nz * nx
    items, depth = features.shape
    levels, rows_own, width = codebook.shape
    cap = 2 * items // owners
    slots = owners * cap
    hid = w_in.shape[1]
    in_rows, out_rows = w_in.shape[0], w_out.shape[0]
    items_all = items * owners
    hy = ny // ns

    slot_all, payload = ask(codes, codes.T, w_in, w_out, nz, nx, ns, rows_own, cap)
    got_z = exchange(payload, "z")
    w_z, digits = got_z[:, :in_rows + out_rows], got_z[:, in_rows + out_rows:, :slots // nz]
    feats = [features, shift(features, "y", 1), shift(features, "y", 2), shift(features, "y", -1)]
    near = [w_z, shift(w_z, "x", 1), shift(w_z, "x", 2), shift(w_z, "x", -1)]
    other = [shift(block, "s", 1) for block in near]
    steps = jnp.arange(ny, dtype=I32)
    x_place = (x - steps) % nx
    y_place = (y - steps - hy * s) % ny
    y_send = (y + steps - hy * s) % ny
    x_send = (x + steps) % nx

    slot_list = [slot_all[l] for l in range(levels)]
    slot_ids = jnp.arange(slots)
    digit_by = [
        digits, shift(digits, "x", 1), shift(digits, "x", 2), shift(digits, "x", -1)]
    none = jnp.zeros_like(digits)
    by_x = jnp.stack([
        sum(jnp.where((x - k) % nx == xa, digit_by[k], none) for k in range(nx)) for xa in range(nx)])
    far_x = shift(by_x, "s", 1)
    by_sx = jnp.stack([jnp.where(s == sa, by_x, far_x) for sa in range(ns)])
    mine = ((x * ns + s) * cap + jnp.arange(cap))[None, :] == jnp.arange(slots // nz)[:, None]
    picked = mm(by_sx.reshape(-1, slots // nz), mine.astype(BF)).reshape(ns, nx, nz, -1, cap)
    picked = jnp.transpose(picked, (3, 0, 2, 1, 4)).reshape(-1, slots).astype(jnp.int32)
    asked_list = [picked[2 * l] * 32 + picked[2 * l + 1] - 1 for l in range(levels)]
    row_ids = jnp.arange(rows_own)
    rows_out = [
        mm((asked_list[l][:, None] == row_ids[None, :]).astype(BF), codebook[l]).astype(BF).reshape(owners, cap, width)
        for l in range(levels)
    ]
    rows_back = exchange(jnp.concatenate(rows_out, axis=1), OWN)
    words = [
        mm(
            (slot_list[l][:, None] == slot_ids[None, :]).astype(BF),
            rows_back[:, l * cap:(l + 1) * cap].reshape(slots, width),
        )
        for l in range(levels)
    ]

    hidden, slope, w_out_all, *lat = encode(
        feats, near, other, jnp.concatenate([x_place, y_place, y_send]), in_rows, out_rows
    )
    far = shift(lat[2], "y", 2)
    fwd = shift(lat[1], "y", 1)
    bwd = shift(lat[3], "y", -1)
    feats_here, feats_there = turn(feats, y_place)
    words = lax.optimization_barrier(words)
    latent = lat[0] + fwd + bwd + far

    residual = latent
    pull_sum = jnp.zeros_like(latent)
    outgoing = []
    for l in range(levels):
        placed = mm((slot_ids[:, None] == slot_list[l][None, :]).astype(BF), residual.astype(BF))
        outgoing.append(placed.astype(BF).reshape(owners, cap, width))
        residual = residual - words[l]
        pull_sum = pull_sum + residual
    latent_grad = (
        (decoder_grad.astype(F32) + 2.0 * BETA * pull_sum) / jnp.sqrt(F32(items_all))
    ).astype(BF)
    grads = [latent_grad, shift(latent_grad, "y", 1), shift(latent_grad, "y", 2), shift(latent_grad, "y", -1)]
    incoming = exchange(jnp.concatenate(outgoing, axis=1), OWN)
    code_sums = jnp.stack([
        mm(
            (row_ids[:, None] == asked_list[l][None, :]).astype(BF),
            incoming[:, l * cap:(l + 1) * cap].reshape(slots, width),
        )
        for l in range(levels)
    ])

    pre_grad, out_part = back(grads, hidden, slope, w_out_all, y_place)
    out_came = shift(out_part, "s", 1)
    pieces = 2
    step = hid // pieces
    there_rows = feats_there.reshape(hy * depth, items)
    sends = []
    for c in range(pieces):
        there = mm(there_rows, pre_grad[:, c * step:(c + 1) * step])
        came = shift(there, "s", 1)
        sends.append(cut_by_x(feats_here, pre_grad, came, out_part, out_came, x_send, nz, nx, c))
    in_list, out_list = [], []
    for c in range(pieces):
        own, to_1, to_2, to_3 = sends[c]
        sum_x = (
            own
            + shift(to_1, "x", 1).astype(F32)
            + shift(to_2, "x", 2).astype(F32)
            + shift(to_3, "x", -1).astype(F32)
        )
        over_z = exchange(sum_x.astype(BF), "z")
        sum_z = jnp.sum(over_z.astype(F32), axis=0)
        in_list.append(sum_z[:in_rows])
        out_list.append(sum_z[in_rows:])
    return (jnp.concatenate(in_list, axis=1), jnp.concatenate(out_list, axis=1), code_sums)


def solution(mesh):
    fine = Mesh(mesh.devices.reshape(2, 8, 4, 4), ("s", "z", "x", "y"))
    in_specs = (
        P(OWN, "y"),
        P(OWN, "y"),
        P(OWN, "y"),
        P(None, OWN, "y"),
        P(None, OWN),
        P(OWN, "y"),
    )
    out_specs = (P(OWN, "y"), P(OWN, "y"), P(None, OWN, "y"))
    return jax.shard_map(shards, mesh=fine, in_specs=in_specs, out_specs=out_specs, check_vma=False)
```

```python
import jax
import jax.numpy as jnp
from jax import lax
from jax.experimental import pallas as pl
from jax.experimental.pallas import tpu as pltpu
from jax.sharding import Mesh, PartitionSpec as P

BETA = 0.25
BF = jnp.bfloat16
F32 = jnp.float32
I32 = jnp.int32
OWN = ("s", "z", "x")
VMEM = pl.BlockSpec(memory_space=pltpu.VMEM)
SMEM = pl.BlockSpec(memory_space=pltpu.SMEM)


def shift(value, axis, by):
    size = lax.axis_size(axis)
    return lax.ppermute(value, axis, [(i, (i + by) % size) for i in range(size)])


def exchange(value, axis):
    return lax.all_to_all(value, axis, split_axis=0, concat_axis=0, tiled=True)


def mm(a, b, dims=((1,), (0,))):
    return lax.dot_general(a, b, (dims, ((), ())), preferred_element_type=F32)


def encode(feats, near, other, place, in_rows, out_rows):
    items, depth = feats[0].shape
    nz, _, hid = near[0].shape
    nx = len(near)
    ny = len(feats)
    hz = nz * 2 // ny
    width = hz * nx * out_rows
    tile = items // 2

    def kernel(place_ref, *refs):
        f_refs, refs = refs[:ny], refs[ny:]
        n_refs, refs = refs[:nx], refs[nx:]
        o_refs, refs = refs[:nx], refs[nx:]
        hid_ref, slope_ref, wo_ref = refs[:3]
        lat_refs, (w_ref, wo32_ref) = refs[3:3 + ny], refs[3 + ny:]
        for k in range(nx):
            xk = place_ref[k]
            for r, ref in enumerate((n_refs[k], o_refs[k])):
                for zh in range(ny // 2):
                    p = r * (ny // 2) + zh
                    cut = ref[zh * hz:(zh + 1) * hz]
                    w_ref[p, :, xk] = cut[:, :in_rows]
                    wo32_ref[p, :, xk] = cut[:, in_rows:].astype(F32)
        for p in range(ny):
            wo_ref[p] = wo32_ref[p].reshape(width, hid).astype(BF)

        def step(t, carry):
            rows = pl.ds(t * tile, tile)
            acc = None
            for k in range(ny):
                part = mm(f_refs[k][rows, :], w_ref[place_ref[nx + k]].reshape(depth, hid))
                acc = part if acc is None else acc + part
            logistic = jax.nn.sigmoid(acc)
            hidden = (acc * logistic).astype(BF)
            hid_ref[rows, :] = hidden
            slope_ref[rows, :] = logistic * (1.0 + acc * (1.0 - logistic))
            for j in range(ny):
                lat_refs[j][rows, :] = mm(hidden, wo_ref[place_ref[nx + ny + j]], ((1,), (1,)))
            return carry

        lax.fori_loop(0, items // tile, step, 0)

    return pl.pallas_call(
        kernel,
        out_shape=[
            jax.ShapeDtypeStruct((items, hid), BF),
            jax.ShapeDtypeStruct((items, hid), F32),
            jax.ShapeDtypeStruct((ny, width, hid), BF),
        ] + [jax.ShapeDtypeStruct((items, width), F32)] * ny,
        in_specs=[SMEM] + [VMEM] * (ny + 2 * nx),
        out_specs=[VMEM] * (3 + ny),
        scratch_shapes=[
            pltpu.VMEM((ny, hz, nx, in_rows, hid), BF),
            pltpu.VMEM((ny, hz, nx, out_rows, hid), F32),
        ],
        compiler_params=pltpu.CompilerParams(vmem_limit_bytes=48 * 1024 * 1024),
        cost_estimate=pl.CostEstimate(
            flops=2 * items * hid * ny * (depth + width), bytes_accessed=12 << 20, transcendentals=items * hid),
        name="encode",
    )(place, *feats, *near, *other)


def ask(codes, w_in, w_out, nz, nx, ns, rows_own, cap):
    levels, items = codes.shape
    in_rows, hid = w_in.shape
    out_rows = w_out.shape[0]
    owners = ns * nz * nx
    slots = owners * cap
    group = slots // nz
    digit_rows = 8
    lane = 128

    def kernel(codes_ref, wi_ref, wo_ref, slot_ref, pay_ref, col_ref, found_ref):
        fill = jnp.zeros((8 - levels, lane), I32)
        for t in range(items // lane):
            block = jnp.concatenate([codes_ref[:, t * lane:(t + 1) * lane], fill], axis=0).T
            for l in range(levels):
                col_ref[l, t * lane:(t + 1) * lane, :] = block[:, l:l + 1]
        found_ref[...] = jnp.zeros_like(found_ref)

        def level(l, carry):
            code_row, code_col = codes_ref[pl.ds(l, 1), :], col_ref[l]
            own_row, own_col = code_row // rows_own, code_col // rows_own
            first = lax.broadcasted_iota(I32, (items, items), 0)
            second = lax.broadcasted_iota(I32, (items, items), 1)
            before = jnp.where(second < first, jnp.where(own_col == own_row, 1.0, 0.0), 0.0)
            rank = jnp.sum(before, axis=1, keepdims=True).astype(I32)
            slot_ref[l] = own_col * cap + rank
            section, rest = own_col // (nz * nx), own_col % (nz * nx)
            spot = (rest * ns + section) * cap + rank
            value = (code_col % rows_own + 1).astype(F32)
            lanes = lax.broadcasted_iota(I32, (items, slots), 1)
            want = jnp.sum(jnp.where(lanes == spot, value, 0.0), axis=0, keepdims=True).astype(I32)
            found_ref[pl.ds(2 * l, 1), :] = (want // 32).astype(F32)
            found_ref[pl.ds(2 * l + 1, 1), :] = (want % 32).astype(F32)
            return carry

        lax.fori_loop(0, levels, level, 0)
        rest = jnp.zeros((digit_rows, hid - group), F32)
        for z in range(nz):
            pay_ref[z, :in_rows] = wi_ref[...]
            digits = jnp.concatenate([found_ref[:, z * group:(z + 1) * group], rest], axis=1)
            pay_ref[z, in_rows:] = jnp.concatenate([wo_ref[...].astype(F32), digits], axis=0).astype(BF)

    return pl.pallas_call(
        kernel,
        out_shape=[
            jax.ShapeDtypeStruct((levels, items, 1), I32),
            jax.ShapeDtypeStruct((nz, in_rows + out_rows + digit_rows, hid), BF),
        ],
        in_specs=[VMEM] * 3,
        out_specs=[VMEM] * 2,
        scratch_shapes=[pltpu.VMEM((levels, items, 1), I32), pltpu.VMEM((digit_rows, slots), F32)],
        name="ask",
    )(codes, w_in, w_out)


def pick(asked, book, owners):
    levels, lines, lane = asked.shape
    rows_own, width = book.shape[1:]
    slots = lines * lane
    cap = slots // owners
    tile = 256

    def kernel(asked_ref, book_ref, out_ref, col_ref):
        turned = asked_ref[0].T
        for t in range(lines):
            col_ref[t * lane:(t + 1) * lane, :] = turned[:, t:t + 1]

        def step(t, carry):
            col = col_ref[pl.ds(pl.multiple_of(t * tile, tile), tile), :]
            hit = jnp.where(lax.broadcasted_iota(I32, (tile, rows_own), 1) == col, 1.0, 0.0).astype(BF)
            got = mm(hit, book_ref[0]).astype(BF)
            out_ref[pl.ds(t * (tile // cap), tile // cap)] = got.reshape(tile // cap, cap, width)
            return carry

        lax.fori_loop(0, slots // tile, step, 0)

    return pl.pallas_call(
        kernel,
        out_shape=jax.ShapeDtypeStruct((owners, levels * cap, width), BF),
        grid=(levels,),
        in_specs=[
            pl.BlockSpec((1, lines, lane), lambda l: (l, 0, 0)),
            pl.BlockSpec((1, rows_own, width), lambda l: (l, 0, 0)),
        ],
        out_specs=pl.BlockSpec((owners, cap, width), lambda l: (0, l, 0)),
        scratch_shapes=[pltpu.VMEM((slots, 1), I32)],
        name="pick",
    )(asked, book)


def collect(asked, incoming, rows_own):
    levels, lines, lane = asked.shape
    owners, _, width = incoming.shape
    slots = lines * lane
    cap = slots // owners
    tile = 256

    def kernel(asked_ref, in_ref, out_ref):
        line = jnp.concatenate([asked_ref[0, t:t + 1, :] for t in range(lines)], axis=1)
        values = in_ref[...].reshape(slots, width)

        def step(t, carry):
            rows = lax.broadcasted_iota(I32, (tile, slots), 0) + t * tile
            hit = jnp.where(rows == line, 1.0, 0.0).astype(BF)
            out_ref[0, pl.ds(pl.multiple_of(t * tile, tile), tile), :] = mm(hit, values)
            return carry

        lax.fori_loop(0, rows_own // tile, step, 0)

    return pl.pallas_call(
        kernel,
        out_shape=jax.ShapeDtypeStruct((levels, rows_own, width), F32),
        grid=(levels,),
        in_specs=[
            pl.BlockSpec((1, lines, lane), lambda l: (l, 0, 0)),
            pl.BlockSpec((owners, cap, width), lambda l: (0, l, 0)),
        ],
        out_specs=pl.BlockSpec((1, rows_own, width), lambda l: (l, 0, 0)),
        name="collect",
    )(asked, incoming)


def turn(feats, place):
    items, depth = feats[0].shape
    ny = len(feats)
    hy = ny // 2
    cols = 256

    def kernel(place_ref, *refs):
        here_ref, there_ref = refs[ny:]
        for k in range(ny):
            spot = place_ref[k]
            flat = refs[k][...].T

            @pl.when(spot < hy)
            def _():
                here_ref[spot] = flat

            @pl.when(spot >= hy)
            def _():
                there_ref[spot - hy] = flat

    out = pl.BlockSpec((hy, cols, items), lambda i: (0, i, 0))
    return pl.pallas_call(
        kernel,
        out_shape=[jax.ShapeDtypeStruct((hy, depth, items), BF)] * 2,
        grid=(depth // cols,),
        in_specs=[SMEM] + [pl.BlockSpec((items, cols), lambda i: (0, i))] * ny,
        out_specs=[out] * 2,
        cost_estimate=pl.CostEstimate(flops=0, bytes_accessed=8 << 20, transcendentals=0),
        name="turn",
    )(place, *feats)


def back(grads, hidden, slope, w_out, place):
    items, hid = hidden.shape
    ny, width = w_out.shape[:2]

    def kernel(place_ref, *refs):
        g_refs, (hid_ref, slope_ref, wo_ref, pre_ref, out_ref) = refs[:ny], refs[ny:]
        acc = None
        for k in range(ny):
            part = mm(g_refs[k][...], wo_ref[place_ref[k]])
            acc = part if acc is None else acc + part
            out_ref[place_ref[k]] = mm(g_refs[k][...], hid_ref[...], ((0,), (0,)))
        pre_ref[...] = (acc * slope_ref[...]).astype(BF)

    return pl.pallas_call(
        kernel,
        out_shape=[
            jax.ShapeDtypeStruct((items, hid), BF),
            jax.ShapeDtypeStruct((ny, width, hid), F32),
        ],
        in_specs=[SMEM] + [VMEM] * (ny + 3),
        out_specs=[VMEM] * 2,
        cost_estimate=pl.CostEstimate(flops=4 * items * hid * ny * width, bytes_accessed=4 << 20, transcendentals=0),
        name="back",
    )(place, *grads, hidden, slope, w_out)


def cut_by_x(feats_t, pre, came, out_mine, out_came, order, nz, nx, c):
    items = feats_t.shape[2]
    hid = came.shape[1]
    in_rows = came.shape[0] // (nz * nx)
    hy = feats_t.shape[0]
    ny, width = out_mine.shape[:2]
    out_rows = hy * width // (nz * nx)
    both = in_rows + out_rows
    feats_t = feats_t.reshape(-1, items)
    out_mine = out_mine.reshape(ny * width, -1)
    out_came = out_came.reshape(ny * width, -1)
    group = 2
    many, few = group * nx * in_rows, group * nx * out_rows
    ahead = hy * width // few

    def kernel(order_ref, f_ref, p_ref, came_ref, om_ref, oc_ref, own_ref, *rest):
        sends, part = rest[:-1], rest[-1]
        total = (mm(f_ref[...], p_ref[...]) + came_ref[...]).reshape(group, nx, in_rows, hid)
        outs = (om_ref[...] + oc_ref[...]).reshape(group, nx, out_rows, hid)
        for g in range(group):
            part[:, :in_rows] = total[g]
            part[:, in_rows:] = outs[g]
            own_ref[g] = part[order_ref[0]]
            for k, send in enumerate(sends):
                send[g] = part[order_ref[k + 1]].astype(BF)

    block = pl.BlockSpec((group, both, hid), lambda t: (t, 0, 0))
    return pl.pallas_call(
        kernel,
        out_shape=[jax.ShapeDtypeStruct((nz, both, hid), F32)]
        + [jax.ShapeDtypeStruct((nz, both, hid), BF)] * (nx - 1),
        grid=(nz // group,),
        in_specs=[
            SMEM,
            pl.BlockSpec((many, items), lambda t: (t, 0)),
            pl.BlockSpec((items, hid), lambda t: (0, c)),
            pl.BlockSpec((many, hid), lambda t: (t, 0)),
            pl.BlockSpec((few, hid), lambda t: (t, c)),
            pl.BlockSpec((few, hid), lambda t: (ahead + t, c)),
        ],
        out_specs=[block] * nx,
        scratch_shapes=[pltpu.VMEM((nx, both, hid), F32)],
        cost_estimate=pl.CostEstimate(
            flops=2 * nz * nx * in_rows * items * hid, bytes_accessed=8 << 20, transcendentals=0),
        name="cut_by_x",
    )(order, feats_t, pre, came, out_mine, out_came)


def shards(features, w_in, w_out, codebook, codes, decoder_grad):
    s, x, y = lax.axis_index("s"), lax.axis_index("x"), lax.axis_index("y")
    ns, nz, nx, ny = (lax.axis_size(a) for a in ("s", "z", "x", "y"))
    owners = ns * nz * nx
    items, depth = features.shape
    levels, rows_own, width = codebook.shape
    cap = 2 * items // owners
    slots = owners * cap
    hid = w_in.shape[1]
    in_rows, out_rows = w_in.shape[0], w_out.shape[0]
    items_all = items * owners
    hy = ny // ns

    slot_all, payload = ask(codes, w_in, w_out, nz, nx, ns, rows_own, cap)
    got_z = exchange(payload, "z")
    w_z, digits = got_z[:, :in_rows + out_rows], got_z[:, in_rows + out_rows:, :slots // nz]
    feats = [features, shift(features, "y", 1), shift(features, "y", 2), shift(features, "y", -1)]
    near = [w_z, shift(w_z, "x", 1), shift(w_z, "x", 2), shift(w_z, "x", -1)]
    other = [shift(block, "s", 1) for block in near]
    steps = jnp.arange(ny, dtype=I32)
    x_place = (x - steps) % nx
    y_place = (y - steps - hy * s) % ny
    y_send = (y + steps - hy * s) % ny
    x_send = (x + steps) % nx

    slot_list = [slot_all[l, :, 0] for l in range(levels)]
    slot_ids = jnp.arange(slots)
    digit_by = [
        digits, shift(digits, "x", 1), shift(digits, "x", 2), shift(digits, "x", -1)]
    none = jnp.zeros_like(digits)
    by_x = jnp.stack([
        sum(jnp.where((x - k) % nx == xa, digit_by[k], none) for k in range(nx)) for xa in range(nx)])
    far_x = shift(by_x, "s", 1)
    by_sx = jnp.stack([jnp.where(s == sa, by_x, far_x) for sa in range(ns)])
    mine = ((x * ns + s) * cap + jnp.arange(cap))[None, :] == jnp.arange(slots // nz)[:, None]
    picked = mm(by_sx.reshape(-1, slots // nz), mine.astype(BF)).reshape(ns, nx, nz, -1, cap)
    picked = jnp.transpose(picked, (3, 0, 2, 1, 4)).reshape(-1, slots).astype(jnp.int32)
    asked = (picked[0::2] * 32 + picked[1::2] - 1)[:levels].reshape(levels, -1, 128)
    rows_back = exchange(pick(asked, codebook, owners), OWN)
    words = [
        mm(
            (slot_list[l][:, None] == slot_ids[None, :]).astype(BF),
            rows_back[:, l * cap:(l + 1) * cap].reshape(slots, width),
        )
        for l in range(levels)
    ]

    hidden, slope, w_out_all, *lat = encode(
        feats, near, other, jnp.concatenate([x_place, y_place, y_send]), in_rows, out_rows
    )
    far = shift(lat[2], "y", 2)
    fwd = shift(lat[1], "y", 1)
    bwd = shift(lat[3], "y", -1)
    feats_here, feats_there = turn(feats, y_place)
    words = lax.optimization_barrier(words)
    latent = lat[0] + fwd + bwd + far

    residual = latent
    pull_sum = jnp.zeros_like(latent)
    outgoing = []
    for l in range(levels):
        placed = mm((slot_ids[:, None] == slot_list[l][None, :]).astype(BF), residual.astype(BF))
        outgoing.append(placed.astype(BF).reshape(owners, cap, width))
        residual = residual - words[l]
        pull_sum = pull_sum + residual
    latent_grad = (
        (decoder_grad.astype(F32) + 2.0 * BETA * pull_sum) / jnp.sqrt(F32(items_all))
    ).astype(BF)
    grads = [
        latent_grad,
        shift(latent_grad, "y", 1),
        shift(latent_grad, "y", 2),
        shift(latent_grad, "y", -1),
    ]
    incoming = exchange(jnp.concatenate(outgoing, axis=1), OWN)
    code_sums = collect(asked, incoming, rows_own)

    pre_grad, out_part = back(grads, hidden, slope, w_out_all, y_place)
    out_came = shift(out_part, "s", 1)
    pieces = 2
    step = hid // pieces
    there_rows = feats_there.reshape(hy * depth, items)
    sends = []
    for c in range(pieces):
        there = mm(there_rows, pre_grad[:, c * step:(c + 1) * step])
        came = shift(there, "s", 1)
        sends.append(cut_by_x(feats_here, pre_grad, came, out_part, out_came, x_send, nz, nx, c))
    in_list, out_list = [], []
    for c in range(pieces):
        own, to_1, to_2, to_3 = sends[c]
        sum_x = (
            own
            + shift(to_1, "x", 1).astype(F32)
            + shift(to_2, "x", 2).astype(F32)
            + shift(to_3, "x", -1).astype(F32)
        )
        over_z = exchange(sum_x.astype(BF), "z")
        sum_z = jnp.sum(over_z.astype(F32), axis=0)
        in_list.append(sum_z[:in_rows])
        out_list.append(sum_z[in_rows:])
    return (jnp.concatenate(in_list, axis=1), jnp.concatenate(out_list, axis=1), code_sums)


def solution(mesh):
    fine = Mesh(mesh.devices.reshape(2, 8, 4, 4), ("s", "z", "x", "y"))
    in_specs = (
        P(OWN, "y"),
        P(OWN, "y"),
        P(OWN, "y"),
        P(None, OWN, "y"),
        P(None, OWN),
        P(OWN, "y"),
    )
    out_specs = (P(OWN, "y"), P(OWN, "y"), P(None, OWN, "y"))
    return jax.shard_map(shards, mesh=fine, in_specs=in_specs, out_specs=out_specs, check_vma=False)
```

```python
import jax
import jax.numpy as jnp
from jax import lax
from jax.experimental import pallas as pl
from jax.experimental.pallas import tpu as pltpu
from jax.sharding import Mesh, PartitionSpec as P

BETA = 0.25
BF = jnp.bfloat16
F32 = jnp.float32
I32 = jnp.int32
OWN = ("s", "z", "x")
VMEM = pl.BlockSpec(memory_space=pltpu.VMEM)
SMEM = pl.BlockSpec(memory_space=pltpu.SMEM)


def shift(value, axis, by):
    size = lax.axis_size(axis)
    return lax.ppermute(value, axis, [(i, (i + by) % size) for i in range(size)])


def exchange(value, axis):
    return lax.all_to_all(value, axis, split_axis=0, concat_axis=0, tiled=True)


def mm(a, b, dims=((1,), (0,))):
    return lax.dot_general(a, b, (dims, ((), ())), preferred_element_type=F32)


def split(value, size):
    if size & (size - 1) == 0:
        return lax.shift_right_logical(value, jnp.full_like(value, size.bit_length() - 1)), value & (size - 1)
    return value // size, value % size


def encode(feats, near, other, spans, place, in_rows, out_rows):
    items, depth = feats[0].shape
    nz, _, hid = near[0].shape
    many = len(near)
    nx = 1 + max(k for k, _, _ in spans)
    ny = len(feats)
    hz = nz * 2 // ny
    width = hz * nx * out_rows
    tile = items // 2

    def kernel(place_ref, *refs):
        f_refs, refs = refs[:ny], refs[ny:]
        n_refs, refs = refs[:many], refs[many:]
        o_refs, refs = refs[:many], refs[many:]
        hid_ref, slope_ref, wo_ref = refs[:3]
        lat_refs, (w_ref, wo32_ref) = refs[3:3 + ny], refs[3 + ny:]
        for (k, low, high), *pair in zip(spans, n_refs, o_refs):
            xk = place_ref[k]
            for r, ref in enumerate(pair):
                for zh in range(low, high):
                    p = r * (ny // 2) + zh
                    cut = ref[(zh - low) * hz:(zh - low + 1) * hz]
                    w_ref[p, :, xk] = cut[:, :in_rows]
                    wo32_ref[p, :, xk] = cut[:, in_rows:].astype(F32)
        for p in range(ny):
            wo_ref[p] = wo32_ref[p].reshape(width, hid).astype(BF)

        def step(t, carry):
            rows = pl.ds(t * tile, tile)
            acc = None
            for k in range(ny):
                part = mm(f_refs[k][rows, :], w_ref[place_ref[nx + k]].reshape(depth, hid))
                acc = part if acc is None else acc + part
            logistic = jax.nn.sigmoid(acc)
            hidden = (acc * logistic).astype(BF)
            hid_ref[rows, :] = hidden
            slope_ref[rows, :] = logistic * (1.0 + acc * (1.0 - logistic))
            for j in range(ny):
                lat_refs[j][rows, :] = mm(hidden, wo_ref[place_ref[nx + ny + j]], ((1,), (1,)))
            return carry

        lax.fori_loop(0, items // tile, step, 0)

    return pl.pallas_call(
        kernel,
        out_shape=[
            jax.ShapeDtypeStruct((items, hid), BF),
            jax.ShapeDtypeStruct((items, hid), F32),
            jax.ShapeDtypeStruct((ny, width, hid), BF),
        ] + [jax.ShapeDtypeStruct((items, width), F32)] * ny,
        in_specs=[SMEM] + [VMEM] * (ny + 2 * many),
        out_specs=[VMEM] * (3 + ny),
        scratch_shapes=[
            pltpu.VMEM((ny, hz, nx, in_rows, hid), BF),
            pltpu.VMEM((ny, hz, nx, out_rows, hid), F32),
        ],
        compiler_params=pltpu.CompilerParams(vmem_limit_bytes=48 * 1024 * 1024),
        cost_estimate=pl.CostEstimate(
            flops=2 * items * hid * ny * (depth + width), bytes_accessed=12 << 20, transcendentals=items * hid),
        name="encode",
    )(place, *feats, *near, *other)


def ask(codes, w_in, w_out, nz, nx, ns, rows_own, cap):
    levels, items = codes.shape
    in_rows, hid = w_in.shape
    out_rows = w_out.shape[0]
    owners = ns * nz * nx
    slots = owners * cap
    group = slots // nz
    digit_rows = 8
    lane = 128

    def kernel(codes_ref, wi_ref, wo_ref, slot_ref, pay_ref, col_ref, found_ref):
        fill = jnp.zeros((8 - levels, lane), I32)
        for t in range(items // lane):
            block = jnp.concatenate([codes_ref[:, t * lane:(t + 1) * lane], fill], axis=0).T
            for l in range(levels):
                col_ref[l, t * lane:(t + 1) * lane, :] = block[:, l:l + 1]
        found_ref[...] = jnp.zeros_like(found_ref)

        def level(l, carry):
            code_row, code_col = codes_ref[pl.ds(l, 1), :], col_ref[l]
            own_row, _ = split(code_row, rows_own)
            own_col, row_col = split(code_col, rows_own)
            first = lax.broadcasted_iota(I32, (items, items), 0)
            second = lax.broadcasted_iota(I32, (items, items), 1)
            before = jnp.where(second < first, jnp.where(own_col == own_row, 1.0, 0.0), 0.0)
            rank = jnp.sum(before, axis=1, keepdims=True).astype(I32)
            slot_ref[l] = own_col * cap + rank
            section, rest = split(own_col, nz * nx)
            spot = (rest * ns + section) * cap + rank
            value = (row_col + 1).astype(F32)
            lanes = lax.broadcasted_iota(I32, (items, slots), 1)
            want = jnp.sum(jnp.where(lanes == spot, value, 0.0), axis=0, keepdims=True).astype(I32)
            high, low = split(want, 32)
            found_ref[pl.ds(2 * l, 1), :] = high.astype(F32)
            found_ref[pl.ds(2 * l + 1, 1), :] = low.astype(F32)
            return carry

        lax.fori_loop(0, levels, level, 0)
        rest = jnp.zeros((digit_rows, hid - group), F32)
        for z in range(nz):
            pay_ref[z, :in_rows] = wi_ref[...]
            digits = jnp.concatenate([found_ref[:, z * group:(z + 1) * group], rest], axis=1)
            pay_ref[z, in_rows:] = jnp.concatenate([wo_ref[...].astype(F32), digits], axis=0).astype(BF)

    return pl.pallas_call(
        kernel,
        out_shape=[
            jax.ShapeDtypeStruct((levels, items, 1), I32),
            jax.ShapeDtypeStruct((nz, in_rows + out_rows + digit_rows, hid), BF),
        ],
        in_specs=[VMEM] * 3,
        out_specs=[VMEM] * 2,
        scratch_shapes=[pltpu.VMEM((levels, items, 1), I32), pltpu.VMEM((digit_rows, slots), F32)],
        name="ask",
    )(codes, w_in, w_out)


def pick(asked, book, owners):
    levels, lines, lane = asked.shape
    rows_own, width = book.shape[1:]
    slots = lines * lane
    cap = slots // owners
    tile = 256

    def kernel(asked_ref, book_ref, out_ref, col_ref):
        turned = asked_ref[0].T
        for t in range(lines):
            col_ref[t * lane:(t + 1) * lane, :] = turned[:, t:t + 1]

        def step(t, carry):
            col = col_ref[pl.ds(pl.multiple_of(t * tile, tile), tile), :]
            hit = jnp.where(lax.broadcasted_iota(I32, (tile, rows_own), 1) == col, 1.0, 0.0).astype(BF)
            got = mm(hit, book_ref[0]).astype(BF)
            out_ref[pl.ds(t * (tile // cap), tile // cap)] = got.reshape(tile // cap, cap, width)
            return carry

        lax.fori_loop(0, slots // tile, step, 0)

    return pl.pallas_call(
        kernel,
        out_shape=jax.ShapeDtypeStruct((owners, levels * cap, width), BF),
        grid=(levels,),
        in_specs=[
            pl.BlockSpec((1, lines, lane), lambda l: (l, 0, 0)),
            pl.BlockSpec((1, rows_own, width), lambda l: (l, 0, 0)),
        ],
        out_specs=pl.BlockSpec((owners, cap, width), lambda l: (0, l, 0)),
        scratch_shapes=[pltpu.VMEM((slots, 1), I32)],
        name="pick",
    )(asked, book)


def collect(asked, incoming, rows_own):
    levels, lines, lane = asked.shape
    owners, _, width = incoming.shape
    slots = lines * lane
    cap = slots // owners
    tile = 256

    def kernel(asked_ref, in_ref, out_ref):
        line = jnp.concatenate([asked_ref[0, t:t + 1, :] for t in range(lines)], axis=1)
        values = in_ref[...].reshape(slots, width)

        def step(t, carry):
            rows = lax.broadcasted_iota(I32, (tile, slots), 0) + t * tile
            hit = jnp.where(rows == line, 1.0, 0.0).astype(BF)
            out_ref[0, pl.ds(pl.multiple_of(t * tile, tile), tile), :] = mm(hit, values)
            return carry

        lax.fori_loop(0, rows_own // tile, step, 0)

    return pl.pallas_call(
        kernel,
        out_shape=jax.ShapeDtypeStruct((levels, rows_own, width), F32),
        grid=(levels,),
        in_specs=[
            pl.BlockSpec((1, lines, lane), lambda l: (l, 0, 0)),
            pl.BlockSpec((owners, cap, width), lambda l: (0, l, 0)),
        ],
        out_specs=pl.BlockSpec((1, rows_own, width), lambda l: (l, 0, 0)),
        name="collect",
    )(asked, incoming)


def turn(feats, place):
    items, depth = feats[0].shape
    ny = len(feats)
    hy = ny // 2
    cols = 256

    def kernel(place_ref, *refs):
        here_ref, there_ref = refs[ny:]
        for k in range(ny):
            spot = place_ref[k]
            flat = refs[k][...].T

            @pl.when(spot < hy)
            def _():
                here_ref[spot] = flat

            @pl.when(spot >= hy)
            def _():
                there_ref[spot - hy] = flat

    out = pl.BlockSpec((hy, cols, items), lambda i: (0, i, 0))
    return pl.pallas_call(
        kernel,
        out_shape=[jax.ShapeDtypeStruct((hy, depth, items), BF)] * 2,
        grid=(depth // cols,),
        in_specs=[SMEM] + [pl.BlockSpec((items, cols), lambda i: (0, i))] * ny,
        out_specs=[out] * 2,
        cost_estimate=pl.CostEstimate(flops=0, bytes_accessed=8 << 20, transcendentals=0),
        name="turn",
    )(place, *feats)


def back(grads, hidden, slope, w_out, place):
    items, hid = hidden.shape
    ny, width = w_out.shape[:2]

    def kernel(place_ref, *refs):
        g_refs, (hid_ref, slope_ref, wo_ref, pre_ref, out_ref) = refs[:ny], refs[ny:]
        acc = None
        for k in range(ny):
            part = mm(g_refs[k][...], wo_ref[place_ref[k]])
            acc = part if acc is None else acc + part
            out_ref[place_ref[k]] = mm(g_refs[k][...], hid_ref[...], ((0,), (0,)))
        pre_ref[...] = (acc * slope_ref[...]).astype(BF)

    return pl.pallas_call(
        kernel,
        out_shape=[
            jax.ShapeDtypeStruct((items, hid), BF),
            jax.ShapeDtypeStruct((ny, width, hid), F32),
        ],
        in_specs=[SMEM] + [VMEM] * (ny + 3),
        out_specs=[VMEM] * 2,
        cost_estimate=pl.CostEstimate(flops=4 * items * hid * ny * width, bytes_accessed=4 << 20, transcendentals=0),
        name="back",
    )(place, *grads, hidden, slope, w_out)


def cut_by_x(feats_t, pre, came, out_mine, out_came, order, nz, nx, c):
    items = feats_t.shape[2]
    hid = came.shape[1]
    in_rows = came.shape[0] // (nz * nx)
    hy = feats_t.shape[0]
    ny, width = out_mine.shape[:2]
    out_rows = hy * width // (nz * nx)
    both = in_rows + out_rows
    feats_t = feats_t.reshape(-1, items)
    out_mine = out_mine.reshape(ny * width, -1)
    out_came = out_came.reshape(ny * width, -1)
    group = 2
    many, few = group * nx * in_rows, group * nx * out_rows
    ahead = hy * width // few

    def kernel(order_ref, f_ref, p_ref, came_ref, om_ref, oc_ref, own_ref, *rest):
        sends, part = rest[:-1], rest[-1]
        total = (mm(f_ref[...], p_ref[...]) + came_ref[...].astype(F32)).reshape(group, nx, in_rows, hid)
        outs = (om_ref[...] + oc_ref[...]).reshape(group, nx, out_rows, hid)
        for g in range(group):
            part[:, :in_rows] = total[g]
            part[:, in_rows:] = outs[g]
            own_ref[g] = part[order_ref[0]]
            for k, send in enumerate(sends):
                send[g] = part[order_ref[k + 1]].astype(BF)

    block = pl.BlockSpec((group, both, hid), lambda t: (t, 0, 0))
    return pl.pallas_call(
        kernel,
        out_shape=[jax.ShapeDtypeStruct((nz, both, hid), F32)]
        + [jax.ShapeDtypeStruct((nz, both, hid), BF)] * (nx - 1),
        grid=(nz // group,),
        in_specs=[
            SMEM,
            pl.BlockSpec((many, items), lambda t: (t, 0)),
            pl.BlockSpec((items, hid), lambda t: (0, c)),
            pl.BlockSpec((many, hid), lambda t: (t, 0)),
            pl.BlockSpec((few, hid), lambda t: (t, c)),
            pl.BlockSpec((few, hid), lambda t: (ahead + t, c)),
        ],
        out_specs=[block] * nx,
        scratch_shapes=[pltpu.VMEM((nx, both, hid), F32)],
        cost_estimate=pl.CostEstimate(
            flops=2 * nz * nx * in_rows * items * hid, bytes_accessed=8 << 20, transcendentals=0),
        name="cut_by_x",
    )(order, feats_t, pre, came, out_mine, out_came)


def finish(parts, in_rows):
    _, both, step = parts[0].shape
    hid = step * len(parts)

    def kernel(*refs):
        in_ref, out_ref = refs[-2:]
        for c, ref in enumerate(refs[:-2]):
            total = jnp.sum(ref[...].astype(F32), axis=0)
            in_ref[:, c * step:(c + 1) * step] = total[:in_rows]
            out_ref[:, c * step:(c + 1) * step] = total[in_rows:]

    return pl.pallas_call(
        kernel,
        out_shape=[jax.ShapeDtypeStruct((in_rows, hid), F32), jax.ShapeDtypeStruct((both - in_rows, hid), F32)],
        in_specs=[VMEM] * len(parts),
        out_specs=[VMEM] * 2,
        name="finish",
    )(*parts)


def shards(features, w_in, w_out, codebook, codes, decoder_grad):
    s, x, y = lax.axis_index("s"), lax.axis_index("x"), lax.axis_index("y")
    ns, nz, nx, ny = (lax.axis_size(a) for a in ("s", "z", "x", "y"))
    owners = ns * nz * nx
    items, depth = features.shape
    levels, rows_own, width = codebook.shape
    cap = 2 * items // owners
    slots = owners * cap
    hid = w_in.shape[1]
    in_rows, out_rows = w_in.shape[0], w_out.shape[0]
    items_all = items * owners
    hy = ny // ns

    slot_all, payload = ask(codes, w_in, w_out, nz, nx, ns, rows_own, cap)
    got_z = exchange(payload, "z")
    w_z, digits = got_z[:, :in_rows + out_rows], got_z[:, in_rows + out_rows:, :slots // nz]
    feats = [features, shift(features, "y", 1), shift(features, "y", 2), shift(features, "y", -1)]
    hz = nz // 2
    from_left, from_right = shift(w_z, "x", 1), shift(w_z, "x", -1)
    near = [w_z, from_left, from_right, shift(from_left[:hz], "x", 1), shift(from_right[hz:], "x", -1)]
    spans = [(0, 0, 2), (1, 0, 2), (3, 0, 2), (2, 0, 1), (2, 1, 2)]
    other = [shift(block, "s", 1) for block in near]
    steps = jnp.arange(ny, dtype=I32)
    x_place = (x - steps) % nx
    y_place = (y - steps - hy * s) % ny
    y_send = (y + steps - hy * s) % ny
    x_send = (x + steps) % nx

    slot_list = [slot_all[l, :, 0] for l in range(levels)]
    slot_ids = jnp.arange(slots)
    digit_by = [
        digits, shift(digits, "x", 1), shift(digits, "x", 2), shift(digits, "x", -1)]
    none = jnp.zeros_like(digits)
    by_x = jnp.stack([
        sum(jnp.where((x - k) % nx == xa, digit_by[k], none) for k in range(nx)) for xa in range(nx)])
    far_x = shift(by_x, "s", 1)
    by_sx = jnp.stack([jnp.where(s == sa, by_x, far_x) for sa in range(ns)])
    mine = ((x * ns + s) * cap + jnp.arange(cap))[None, :] == jnp.arange(slots // nz)[:, None]
    picked = mm(by_sx.reshape(-1, slots // nz), mine.astype(BF)).reshape(ns, nx, nz, -1, cap)
    picked = jnp.transpose(picked, (3, 0, 2, 1, 4)).reshape(-1, slots).astype(jnp.int32)
    asked = (picked[0::2] * 32 + picked[1::2] - 1)[:levels].reshape(levels, -1, 128)
    chosen = pick(asked, codebook, owners)
    rows_back = exchange(chosen, OWN)
    words = [
        mm(
            (slot_list[l][:, None] == slot_ids[None, :]).astype(BF),
            rows_back[:, l * cap:(l + 1) * cap].reshape(slots, width),
        )
        for l in range(levels)
    ]

    hidden, slope, w_out_all, *lat = encode(
        feats, near, other, spans, jnp.concatenate([x_place, y_place, y_send]), in_rows, out_rows
    )
    far = shift(lat[2], "y", 2)
    fwd = shift(lat[1], "y", 1)
    bwd = shift(lat[3], "y", -1)
    feats_here, feats_there = turn(feats, y_place)
    words = lax.optimization_barrier(words)
    latent = lat[0] + fwd + bwd + far

    residual = latent
    pull_sum = jnp.zeros_like(latent)
    outgoing = []
    for l in range(levels):
        placed = mm((slot_ids[:, None] == slot_list[l][None, :]).astype(BF), residual.astype(BF))
        outgoing.append(placed.astype(BF).reshape(owners, cap, width))
        residual = residual - words[l]
        pull_sum = pull_sum + residual
    latent_grad = (
        (decoder_grad.astype(F32) + 2.0 * BETA * pull_sum) / jnp.sqrt(F32(items_all))
    ).astype(BF)
    grads = [latent_grad, shift(latent_grad, "y", 1), shift(latent_grad, "y", 2), shift(latent_grad, "y", -1)]
    incoming = exchange(jnp.concatenate(outgoing, axis=1), OWN)
    code_sums = collect(asked, incoming, rows_own)

    pre_grad, out_part = back(grads, hidden, slope, w_out_all, y_place)
    out_came = shift(out_part, "s", 1)
    pieces = 2
    step = hid // pieces
    there_rows = feats_there.reshape(hy * depth, items)
    sends = []
    for c in range(pieces):
        there = mm(there_rows, pre_grad[:, c * step:(c + 1) * step]).astype(BF)
        came = shift(there, "s", 1)
        sends.append(cut_by_x(feats_here, pre_grad, came, out_part, out_came, x_send, nz, nx, c))
    over_z = []
    for c in range(pieces):
        own, to_1, to_2, to_3 = sends[c]
        sum_x = (
            own
            + shift(to_1, "x", 1).astype(F32)
            + shift(to_2, "x", 2).astype(F32)
            + shift(to_3, "x", -1).astype(F32)
        )
        over_z.append(exchange(sum_x.astype(BF), "z"))
    in_grad, out_grad = finish(over_z, in_rows)
    return (in_grad, out_grad, code_sums)


def solution(mesh):
    fine = Mesh(mesh.devices.reshape(2, 8, 4, 4), ("s", "z", "x", "y"))
    in_specs = (
        P(OWN, "y"),
        P(OWN, "y"),
        P(OWN, "y"),
        P(None, OWN, "y"),
        P(None, OWN),
        P(OWN, "y"),
    )
    out_specs = (P(OWN, "y"), P(OWN, "y"), P(None, OWN, "y"))
    return jax.shard_map(shards, mesh=fine, in_specs=in_specs, out_specs=out_specs, check_vma=False)
```

```python
import jax
import jax.numpy as jnp
from jax import lax
from jax.experimental import pallas as pl
from jax.experimental.pallas import tpu as pltpu
from jax.sharding import Mesh, PartitionSpec as P

BETA = 0.25
BF = jnp.bfloat16
F32 = jnp.float32
I32 = jnp.int32
OWN = ("s", "z", "x")
VMEM = pl.BlockSpec(memory_space=pltpu.VMEM)
SMEM = pl.BlockSpec(memory_space=pltpu.SMEM)


def shift(value, axis, by):
    size = lax.axis_size(axis)
    return lax.ppermute(value, axis, [(i, (i + by) % size) for i in range(size)])


def exchange(value, axis):
    return lax.all_to_all(value, axis, split_axis=0, concat_axis=0, tiled=True)


def mm(a, b, dims=((1,), (0,))):
    return lax.dot_general(a, b, (dims, ((), ())), preferred_element_type=F32)


def split(value, size):
    if size & (size - 1) == 0:
        return lax.shift_right_logical(value, jnp.full_like(value, size.bit_length() - 1)), value & (size - 1)
    return value // size, value % size


def encode(feats, near, other, spans, place, in_rows, out_rows):
    items, depth = feats[0].shape
    nz, _, hid = near[0].shape
    many = len(near)
    nx = 1 + max(k for k, _, _ in spans)
    ny = len(feats)
    hz = nz * 2 // ny
    width = hz * nx * out_rows
    tile = items // 2

    def kernel(place_ref, *refs):
        f_refs, refs = refs[:ny], refs[ny:]
        n_refs, refs = refs[:many], refs[many:]
        o_refs, refs = refs[:many], refs[many:]
        hid_ref, slope_ref, wo_ref = refs[:3]
        lat_refs, (w_ref, wo32_ref) = refs[3:3 + ny], refs[3 + ny:]
        for (k, low, high), *pair in zip(spans, n_refs, o_refs):
            xk = place_ref[k]
            for r, ref in enumerate(pair):
                for zh in range(low, high):
                    p = r * (ny // 2) + zh
                    cut = ref[(zh - low) * hz:(zh - low + 1) * hz]
                    w_ref[p, :, xk] = cut[:, :in_rows]
                    wo32_ref[p, :, xk] = cut[:, in_rows:].astype(F32)
        for p in range(ny):
            wo_ref[p] = wo32_ref[p].reshape(width, hid).astype(BF)

        def step(t, carry):
            rows = pl.ds(t * tile, tile)
            acc = None
            for k in range(ny):
                part = mm(f_refs[k][rows, :], w_ref[place_ref[nx + k]].reshape(depth, hid))
                acc = part if acc is None else acc + part
            logistic = jax.nn.sigmoid(acc)
            hidden = (acc * logistic).astype(BF)
            hid_ref[rows, :] = hidden
            slope_ref[rows, :] = logistic * (1.0 + acc * (1.0 - logistic))
            for j in range(ny):
                lat_refs[j][rows, :] = mm(hidden, wo_ref[place_ref[nx + ny + j]], ((1,), (1,)))
            return carry

        lax.fori_loop(0, items // tile, step, 0)

    return pl.pallas_call(
        kernel,
        out_shape=[
            jax.ShapeDtypeStruct((items, hid), BF),
            jax.ShapeDtypeStruct((items, hid), F32),
            jax.ShapeDtypeStruct((ny, width, hid), BF),
        ] + [jax.ShapeDtypeStruct((items, width), F32)] * ny,
        in_specs=[SMEM] + [VMEM] * (ny + 2 * many),
        out_specs=[VMEM] * (3 + ny),
        scratch_shapes=[
            pltpu.VMEM((ny, hz, nx, in_rows, hid), BF),
            pltpu.VMEM((ny, hz, nx, out_rows, hid), F32),
        ],
        compiler_params=pltpu.CompilerParams(vmem_limit_bytes=48 * 1024 * 1024),
        cost_estimate=pl.CostEstimate(
            flops=2 * items * hid * ny * (depth + width), bytes_accessed=12 << 20, transcendentals=items * hid),
        name="encode",
    )(place, *feats, *near, *other)


def ask(codes, w_in, w_out, nz, nx, ns, rows_own, cap):
    levels, items = codes.shape
    in_rows, hid = w_in.shape
    out_rows = w_out.shape[0]
    owners = ns * nz * nx
    slots = owners * cap
    group = slots // nz
    digit_rows = 8
    lane = 128

    def kernel(codes_ref, wi_ref, wo_ref, slot_ref, pay_ref, col_ref, found_ref):
        fill = jnp.zeros((8 - levels, lane), I32)
        for t in range(items // lane):
            block = jnp.concatenate([codes_ref[:, t * lane:(t + 1) * lane], fill], axis=0).T
            for l in range(levels):
                col_ref[l, t * lane:(t + 1) * lane, :] = block[:, l:l + 1]
        found_ref[...] = jnp.zeros_like(found_ref)

        def level(l, carry):
            code_row, code_col = codes_ref[pl.ds(l, 1), :], col_ref[l]
            own_row, _ = split(code_row, rows_own)
            own_col, row_col = split(code_col, rows_own)
            first = lax.broadcasted_iota(I32, (items, items), 0)
            second = lax.broadcasted_iota(I32, (items, items), 1)
            before = jnp.where(second < first, jnp.where(own_col == own_row, 1.0, 0.0), 0.0)
            rank = jnp.sum(before, axis=1, keepdims=True).astype(I32)
            slot_ref[l] = own_col * cap + rank
            section, rest = split(own_col, nz * nx)
            spot = (rest * ns + section) * cap + rank
            value = (row_col + 1).astype(F32)
            lanes = lax.broadcasted_iota(I32, (items, slots), 1)
            want = jnp.sum(jnp.where(lanes == spot, value, 0.0), axis=0, keepdims=True).astype(I32)
            high, low = split(want, 32)
            found_ref[pl.ds(2 * l, 1), :] = high.astype(F32)
            found_ref[pl.ds(2 * l + 1, 1), :] = low.astype(F32)
            return carry

        lax.fori_loop(0, levels, level, 0)
        rest = jnp.zeros((digit_rows, hid - group), F32)
        for z in range(nz):
            pay_ref[z, :in_rows] = wi_ref[...]
            digits = jnp.concatenate([found_ref[:, z * group:(z + 1) * group], rest], axis=1)
            pay_ref[z, in_rows:] = jnp.concatenate([wo_ref[...].astype(F32), digits], axis=0).astype(BF)

    return pl.pallas_call(
        kernel,
        out_shape=[
            jax.ShapeDtypeStruct((levels, items, 1), I32),
            jax.ShapeDtypeStruct((nz, in_rows + out_rows + digit_rows, hid), BF),
        ],
        in_specs=[VMEM] * 3,
        out_specs=[VMEM] * 2,
        scratch_shapes=[pltpu.VMEM((levels, items, 1), I32), pltpu.VMEM((digit_rows, slots), F32)],
        name="ask",
    )(codes, w_in, w_out)


def pick(asked, book, owners):
    levels, lines, lane = asked.shape
    rows_own, width = book.shape[1:]
    slots = lines * lane
    cap = slots // owners
    tile = 256

    def kernel(asked_ref, book_ref, out_ref, col_ref):
        turned = asked_ref[0].T
        for t in range(lines):
            col_ref[t * lane:(t + 1) * lane, :] = turned[:, t:t + 1]

        def step(t, carry):
            col = col_ref[pl.ds(pl.multiple_of(t * tile, tile), tile), :]
            hit = jnp.where(lax.broadcasted_iota(I32, (tile, rows_own), 1) == col, 1.0, 0.0).astype(BF)
            got = mm(hit, book_ref[0]).astype(BF)
            out_ref[pl.ds(t * (tile // cap), tile // cap)] = got.reshape(tile // cap, cap, width)
            return carry

        lax.fori_loop(0, slots // tile, step, 0)

    return pl.pallas_call(
        kernel,
        out_shape=jax.ShapeDtypeStruct((owners, levels * cap, width), BF),
        grid=(levels,),
        in_specs=[
            pl.BlockSpec((1, lines, lane), lambda l: (l, 0, 0)),
            pl.BlockSpec((1, rows_own, width), lambda l: (l, 0, 0)),
        ],
        out_specs=pl.BlockSpec((owners, cap, width), lambda l: (0, l, 0)),
        scratch_shapes=[pltpu.VMEM((slots, 1), I32)],
        name="pick",
    )(asked, book)


def collect(asked, incoming, rows_own):
    levels, lines, lane = asked.shape
    owners, _, width = incoming.shape
    slots = lines * lane
    cap = slots // owners
    tile = 256

    def kernel(asked_ref, in_ref, out_ref):
        line = jnp.concatenate([asked_ref[0, t:t + 1, :] for t in range(lines)], axis=1)
        values = in_ref[...].reshape(slots, width)

        def step(t, carry):
            rows = lax.broadcasted_iota(I32, (tile, slots), 0) + t * tile
            hit = jnp.where(rows == line, 1.0, 0.0).astype(BF)
            out_ref[0, pl.ds(pl.multiple_of(t * tile, tile), tile), :] = mm(hit, values)
            return carry

        lax.fori_loop(0, rows_own // tile, step, 0)

    return pl.pallas_call(
        kernel,
        out_shape=jax.ShapeDtypeStruct((levels, rows_own, width), F32),
        grid=(levels,),
        in_specs=[
            pl.BlockSpec((1, lines, lane), lambda l: (l, 0, 0)),
            pl.BlockSpec((owners, cap, width), lambda l: (0, l, 0)),
        ],
        out_specs=pl.BlockSpec((1, rows_own, width), lambda l: (l, 0, 0)),
        name="collect",
    )(asked, incoming)


def turn(feats, place):
    items, depth = feats[0].shape
    ny = len(feats)
    hy = ny // 2
    cols = 256

    def kernel(place_ref, *refs):
        here_ref, there_ref = refs[ny:]
        for k in range(ny):
            spot = place_ref[k]
            flat = refs[k][...].T

            @pl.when(spot < hy)
            def _():
                here_ref[spot] = flat

            @pl.when(spot >= hy)
            def _():
                there_ref[spot - hy] = flat

    out = pl.BlockSpec((hy, cols, items), lambda i: (0, i, 0))
    return pl.pallas_call(
        kernel,
        out_shape=[jax.ShapeDtypeStruct((hy, depth, items), BF)] * 2,
        grid=(depth // cols,),
        in_specs=[SMEM] + [pl.BlockSpec((items, cols), lambda i: (0, i))] * ny,
        out_specs=[out] * 2,
        cost_estimate=pl.CostEstimate(flops=0, bytes_accessed=8 << 20, transcendentals=0),
        name="turn",
    )(place, *feats)


def back(grads, hidden, slope, w_out, feats_there, place, step):
    items, hid = hidden.shape
    ny, width = w_out.shape[:2]
    rows = feats_there.shape[0]

    def kernel(place_ref, *refs):
        g_refs, (hid_ref, slope_ref, wo_ref, f_ref, pre_ref, out_ref, there_ref) = refs[:ny], refs[ny:]
        acc = None
        for k in range(ny):
            part = mm(g_refs[k][...], wo_ref[place_ref[k]])
            acc = part if acc is None else acc + part
        pre_ref[...] = (acc * slope_ref[...]).astype(BF)

        def product(t, carry):
            cut = pl.ds(pl.multiple_of(t * 512, 512), 512)
            there_ref[cut, :] = mm(f_ref[cut, :], pre_ref[:, :step]).astype(BF)
            return carry

        lax.fori_loop(0, rows // 512, product, 0)
        for k in range(ny):
            out_ref[place_ref[k]] = mm(g_refs[k][...], hid_ref[...], ((0,), (0,)))

    return pl.pallas_call(
        kernel,
        out_shape=[
            jax.ShapeDtypeStruct((items, hid), BF),
            jax.ShapeDtypeStruct((ny, width, hid), F32),
            jax.ShapeDtypeStruct((rows, step), BF),
        ],
        in_specs=[SMEM] + [VMEM] * (ny + 4),
        out_specs=[VMEM] * 3,
        cost_estimate=pl.CostEstimate(flops=6 * items * hid * ny * width, bytes_accessed=6 << 20, transcendentals=0),
        name="back",
    )(place, *grads, hidden, slope, w_out, feats_there)


def cut_by_x(feats_t, pre, came, out_mine, out_came, order, nz, nx, c):
    items = feats_t.shape[2]
    hid = came.shape[1]
    in_rows = came.shape[0] // (nz * nx)
    hy = feats_t.shape[0]
    ny, width = out_mine.shape[:2]
    out_rows = hy * width // (nz * nx)
    both = in_rows + out_rows
    feats_t = feats_t.reshape(-1, items)
    out_mine = out_mine.reshape(ny * width, -1)
    out_came = out_came.reshape(ny * width, -1)
    group = 4
    many, few = group * nx * in_rows, group * nx * out_rows
    ahead = hy * width // few

    def kernel(order_ref, f_ref, p_ref, came_ref, om_ref, oc_ref, own_ref, *rest):
        sends, part = rest[:-1], rest[-1]
        total = (mm(f_ref[...], p_ref[...]) + came_ref[...].astype(F32)).reshape(group, nx, in_rows, hid)
        outs = (om_ref[...] + oc_ref[...]).reshape(group, nx, out_rows, hid)
        for g in range(group):
            part[:, :in_rows] = total[g]
            part[:, in_rows:] = outs[g]
            own_ref[g] = part[order_ref[0]]
            for k, send in enumerate(sends):
                send[g] = part[order_ref[k + 1]].astype(BF)

    block = pl.BlockSpec((group, both, hid), lambda t: (t, 0, 0))
    return pl.pallas_call(
        kernel,
        out_shape=[jax.ShapeDtypeStruct((nz, both, hid), F32)]
        + [jax.ShapeDtypeStruct((nz, both, hid), BF)] * (nx - 1),
        grid=(nz // group,),
        in_specs=[
            SMEM,
            pl.BlockSpec((many, items), lambda t: (t, 0)),
            pl.BlockSpec((items, hid), lambda t: (0, c)),
            pl.BlockSpec((many, hid), lambda t: (t, 0)),
            pl.BlockSpec((few, hid), lambda t: (t, c)),
            pl.BlockSpec((few, hid), lambda t: (ahead + t, c)),
        ],
        out_specs=[block] * nx,
        scratch_shapes=[pltpu.VMEM((nx, both, hid), F32)],
        cost_estimate=pl.CostEstimate(
            flops=2 * nz * nx * in_rows * items * hid, bytes_accessed=8 << 20, transcendentals=0),
        name="cut_by_x",
    )(order, feats_t, pre, came, out_mine, out_came)


def shards(features, w_in, w_out, codebook, codes, decoder_grad):
    s, x, y = lax.axis_index("s"), lax.axis_index("x"), lax.axis_index("y")
    ns, nz, nx, ny = (lax.axis_size(a) for a in ("s", "z", "x", "y"))
    owners = ns * nz * nx
    items, depth = features.shape
    levels, rows_own, width = codebook.shape
    cap = 2 * items // owners
    slots = owners * cap
    hid = w_in.shape[1]
    in_rows, out_rows = w_in.shape[0], w_out.shape[0]
    items_all = items * owners
    hy = ny // ns

    slot_all, payload = ask(codes, w_in, w_out, nz, nx, ns, rows_own, cap)
    got_z = exchange(payload, "z")
    w_z, digits = got_z[:, :in_rows + out_rows], got_z[:, in_rows + out_rows:, :slots // nz]
    feats = [features, shift(features, "y", 1), shift(features, "y", 2), shift(features, "y", -1)]
    hz = nz // 2
    from_left, from_right = shift(w_z, "x", 1), shift(w_z, "x", -1)
    near = [w_z, from_left, from_right, shift(from_left[:hz], "x", 1), shift(from_right[hz:], "x", -1)]
    spans = [(0, 0, 2), (1, 0, 2), (3, 0, 2), (2, 0, 1), (2, 1, 2)]
    other = [shift(block, "s", 1) for block in near]
    steps = jnp.arange(ny, dtype=I32)
    x_place = (x - steps) % nx
    y_place = (y - steps - hy * s) % ny
    y_send = (y + steps - hy * s) % ny
    x_send = (x + steps) % nx

    slot_list = [slot_all[l, :, 0] for l in range(levels)]
    slot_ids = jnp.arange(slots)
    digit_by = [
        digits, shift(digits, "x", 1), shift(digits, "x", 2), shift(digits, "x", -1)]
    none = jnp.zeros_like(digits)
    by_x = jnp.stack([
        sum(jnp.where((x - k) % nx == xa, digit_by[k], none) for k in range(nx)) for xa in range(nx)])
    far_x = shift(by_x, "s", 1)
    by_sx = jnp.stack([jnp.where(s == sa, by_x, far_x) for sa in range(ns)])
    mine = ((x * ns + s) * cap + jnp.arange(cap))[None, :] == jnp.arange(slots // nz)[:, None]
    picked = mm(by_sx.reshape(-1, slots // nz), mine.astype(BF)).reshape(ns, nx, nz, -1, cap)
    picked = jnp.transpose(picked, (3, 0, 2, 1, 4)).reshape(-1, slots).astype(jnp.int32)
    asked = (picked[0::2] * 32 + picked[1::2] - 1)[:levels].reshape(levels, -1, 128)
    chosen = pick(asked, codebook, owners)
    rows_back = exchange(chosen, OWN)
    words = [
        mm(
            (slot_list[l][:, None] == slot_ids[None, :]).astype(BF),
            rows_back[:, l * cap:(l + 1) * cap].reshape(slots, width),
        )
        for l in range(levels)
    ]

    hidden, slope, w_out_all, *lat = encode(
        feats, near, other, spans, jnp.concatenate([x_place, y_place, y_send]), in_rows, out_rows
    )
    far = shift(lat[2], "y", 2)
    fwd = shift(lat[1], "y", 1)
    bwd = shift(lat[3], "y", -1)
    feats_here, feats_there = turn(feats, y_place)
    words = lax.optimization_barrier(words)
    latent = lat[0] + fwd + bwd + far

    residual = latent
    pull_sum = jnp.zeros_like(latent)
    outgoing = []
    for l in range(levels):
        placed = mm((slot_ids[:, None] == slot_list[l][None, :]).astype(BF), residual.astype(BF))
        outgoing.append(placed.astype(BF).reshape(owners, cap, width))
        residual = residual - words[l]
        pull_sum = pull_sum + residual
    latent_grad = (
        (decoder_grad.astype(F32) + 2.0 * BETA * pull_sum) / jnp.sqrt(F32(items_all))
    ).astype(BF)
    grads = [latent_grad, shift(latent_grad, "y", 1), shift(latent_grad, "y", 2), shift(latent_grad, "y", -1)]
    incoming = exchange(jnp.concatenate(outgoing, axis=1), OWN)
    code_sums = collect(asked, incoming, rows_own)

    pieces = 2
    step = hid // pieces
    there_rows = feats_there.reshape(hy * depth, items)
    pre_grad, out_part, there_first = back(grads, hidden, slope, w_out_all, there_rows, y_place, step)
    out_came = shift(out_part, "s", 1)
    sums_x = []
    for c in range(pieces):
        there = there_first if c == 0 else mm(there_rows, pre_grad[:, c * step:(c + 1) * step]).astype(BF)
        came = shift(there, "s", 1)
        own, to_1, to_2, to_3 = cut_by_x(feats_here, pre_grad, came, out_part, out_came, x_send, nz, nx, c)
        sum_x = (
            own
            + shift(to_1, "x", 1).astype(F32)
            + shift(to_2, "x", 2).astype(F32)
            + shift(to_3, "x", -1).astype(F32)
        ).astype(BF)
        sums_x.append(sum_x if c == pieces - 1 else lax.optimization_barrier(sum_x))
    over_z = exchange(jnp.concatenate(sums_x, axis=2), "z")
    in_grad = jnp.sum(over_z[:, :in_rows].astype(F32), axis=0)
    out_grad = jnp.sum(over_z[:, in_rows:].astype(F32), axis=0)
    return (in_grad, out_grad, code_sums)


def solution(mesh):
    fine = Mesh(mesh.devices.reshape(2, 8, 4, 4), ("s", "z", "x", "y"))
    in_specs = (
        P(OWN, "y"),
        P(OWN, "y"),
        P(OWN, "y"),
        P(None, OWN, "y"),
        P(None, OWN),
        P(OWN, "y"),
    )
    out_specs = (P(OWN, "y"), P(OWN, "y"), P(None, OWN, "y"))
    return jax.shard_map(shards, mesh=fine, in_specs=in_specs, out_specs=out_specs, check_vma=False)
```

```python
import jax
import jax.numpy as jnp
from jax import lax
from jax.experimental import pallas as pl
from jax.experimental.pallas import tpu as pltpu
from jax.sharding import Mesh, PartitionSpec as P

BETA = 0.25
BF = jnp.bfloat16
F32 = jnp.float32
I32 = jnp.int32
OWN = ("s", "z", "x")
VMEM = pl.BlockSpec(memory_space=pltpu.VMEM)
SMEM = pl.BlockSpec(memory_space=pltpu.SMEM)


def shift(value, axis, by):
    size = lax.axis_size(axis)
    return lax.ppermute(value, axis, [(i, (i + by) % size) for i in range(size)])


def exchange(value, axis):
    return lax.all_to_all(value, axis, split_axis=0, concat_axis=0, tiled=True)


def mm(a, b, dims=((1,), (0,))):
    return lax.dot_general(a, b, (dims, ((), ())), preferred_element_type=F32)


def split(value, size):
    if size & (size - 1) == 0:
        return lax.shift_right_logical(value, jnp.full_like(value, size.bit_length() - 1)), value & (size - 1)
    return value // size, value % size


def encode(feats, near, other, spans, place, in_rows, out_rows):
    items, depth = feats[0].shape
    nz, _, hid = near[0].shape
    many = len(near)
    nx = 1 + max(k for k, _, _ in spans)
    ny = len(feats)
    hz = nz * 2 // ny
    width = hz * nx * out_rows
    tile = items // 2

    def kernel(place_ref, *refs):
        f_refs, refs = refs[:ny], refs[ny:]
        n_refs, refs = refs[:many], refs[many:]
        o_refs, refs = refs[:many], refs[many:]
        hid_ref, slope_ref, wo_ref = refs[:3]
        lat_refs, (w_ref, wo32_ref) = refs[3:3 + ny], refs[3 + ny:]
        for (k, low, high), *pair in zip(spans, n_refs, o_refs):
            xk = place_ref[k]
            for r, ref in enumerate(pair):
                for zh in range(low, high):
                    p = r * (ny // 2) + zh
                    cut = ref[(zh - low) * hz:(zh - low + 1) * hz]
                    w_ref[p, :, xk] = cut[:, :in_rows]
                    wo32_ref[p, :, xk] = cut[:, in_rows:].astype(F32)
        for p in range(ny):
            wo_ref[p] = wo32_ref[p].reshape(width, hid).astype(BF)

        def step(t, carry):
            rows = pl.ds(t * tile, tile)
            acc = None
            for k in range(ny):
                part = mm(f_refs[k][rows, :], w_ref[place_ref[nx + k]].reshape(depth, hid))
                acc = part if acc is None else acc + part
            logistic = jax.nn.sigmoid(acc)
            hidden = (acc * logistic).astype(BF)
            hid_ref[rows, :] = hidden
            slope_ref[rows, :] = logistic * (1.0 + acc * (1.0 - logistic))
            for j in range(ny):
                lat_refs[j][rows, :] = mm(hidden, wo_ref[place_ref[nx + ny + j]], ((1,), (1,)))
            return carry

        lax.fori_loop(0, items // tile, step, 0)

    return pl.pallas_call(
        kernel,
        out_shape=[
            jax.ShapeDtypeStruct((items, hid), BF),
            jax.ShapeDtypeStruct((items, hid), F32),
            jax.ShapeDtypeStruct((ny, width, hid), BF),
        ] + [jax.ShapeDtypeStruct((items, width), F32)] * ny,
        in_specs=[SMEM] + [VMEM] * (ny + 2 * many),
        out_specs=[VMEM] * (3 + ny),
        scratch_shapes=[
            pltpu.VMEM((ny, hz, nx, in_rows, hid), BF),
            pltpu.VMEM((ny, hz, nx, out_rows, hid), F32),
        ],
        compiler_params=pltpu.CompilerParams(vmem_limit_bytes=48 * 1024 * 1024),
        cost_estimate=pl.CostEstimate(
            flops=2 * items * hid * ny * (depth + width), bytes_accessed=12 << 20, transcendentals=items * hid),
        name="encode",
    )(place, *feats, *near, *other)


def ask(codes, w_in, w_out, nz, nx, ns, rows_own, cap):
    levels, items = codes.shape
    in_rows, hid = w_in.shape
    out_rows = w_out.shape[0]
    owners = ns * nz * nx
    slots = owners * cap
    group = slots // nz
    digit_rows = 8
    lane = 128

    def kernel(codes_ref, wi_ref, wo_ref, slot_ref, pay_ref, col_ref, found_ref):
        fill = jnp.zeros((8 - levels, lane), I32)
        for t in range(items // lane):
            block = jnp.concatenate([codes_ref[:, t * lane:(t + 1) * lane], fill], axis=0).T
            for l in range(levels):
                col_ref[l, t * lane:(t + 1) * lane, :] = block[:, l:l + 1]
        found_ref[...] = jnp.zeros_like(found_ref)

        def level(l, carry):
            code_row, code_col = codes_ref[pl.ds(l, 1), :], col_ref[l]
            own_row, _ = split(code_row, rows_own)
            own_col, row_col = split(code_col, rows_own)
            first = lax.broadcasted_iota(I32, (items, items), 0)
            second = lax.broadcasted_iota(I32, (items, items), 1)
            before = jnp.where(second < first, jnp.where(own_col == own_row, 1.0, 0.0), 0.0)
            rank = jnp.sum(before, axis=1, keepdims=True).astype(I32)
            slot_ref[l] = own_col * cap + rank
            section, rest = split(own_col, nz * nx)
            spot = (rest * ns + section) * cap + rank
            value = (row_col + 1).astype(F32)
            lanes = lax.broadcasted_iota(I32, (items, slots), 1)
            want = jnp.sum(jnp.where(lanes == spot, value, 0.0), axis=0, keepdims=True).astype(I32)
            high, low = split(want, 32)
            found_ref[pl.ds(2 * l, 1), :] = high.astype(F32)
            found_ref[pl.ds(2 * l + 1, 1), :] = low.astype(F32)
            return carry

        lax.fori_loop(0, levels, level, 0)
        rest = jnp.zeros((digit_rows, hid - group), F32)
        for z in range(nz):
            pay_ref[z, :in_rows] = wi_ref[...]
            digits = jnp.concatenate([found_ref[:, z * group:(z + 1) * group], rest], axis=1)
            pay_ref[z, in_rows:] = jnp.concatenate([wo_ref[...].astype(F32), digits], axis=0).astype(BF)

    return pl.pallas_call(
        kernel,
        out_shape=[
            jax.ShapeDtypeStruct((levels, items, 1), I32),
            jax.ShapeDtypeStruct((nz, in_rows + out_rows + digit_rows, hid), BF),
        ],
        in_specs=[VMEM] * 3,
        out_specs=[VMEM] * 2,
        scratch_shapes=[pltpu.VMEM((levels, items, 1), I32), pltpu.VMEM((digit_rows, slots), F32)],
        name="ask",
    )(codes, w_in, w_out)


def pick(asked, book, owners):
    levels, lines, lane = asked.shape
    rows_own, width = book.shape[1:]
    slots = lines * lane
    cap = slots // owners
    tile = 256

    def kernel(asked_ref, book_ref, out_ref, col_ref):
        turned = asked_ref[0].T
        for t in range(lines):
            col_ref[t * lane:(t + 1) * lane, :] = turned[:, t:t + 1]

        def step(t, carry):
            col = col_ref[pl.ds(pl.multiple_of(t * tile, tile), tile), :]
            hit = jnp.where(lax.broadcasted_iota(I32, (tile, rows_own), 1) == col, 1.0, 0.0).astype(BF)
            got = mm(hit, book_ref[0]).astype(BF)
            out_ref[pl.ds(t * (tile // cap), tile // cap)] = got.reshape(tile // cap, cap, width)
            return carry

        lax.fori_loop(0, slots // tile, step, 0)

    return pl.pallas_call(
        kernel,
        out_shape=jax.ShapeDtypeStruct((owners, levels * cap, width), BF),
        grid=(levels,),
        in_specs=[
            pl.BlockSpec((1, lines, lane), lambda l: (l, 0, 0)),
            pl.BlockSpec((1, rows_own, width), lambda l: (l, 0, 0)),
        ],
        out_specs=pl.BlockSpec((owners, cap, width), lambda l: (0, l, 0)),
        scratch_shapes=[pltpu.VMEM((slots, 1), I32)],
        name="pick",
    )(asked, book)


def collect(asked, incoming, rows_own):
    levels, lines, lane = asked.shape
    owners, _, width = incoming.shape
    slots = lines * lane
    cap = slots // owners
    tile = 256

    def kernel(asked_ref, in_ref, out_ref):
        line = jnp.concatenate([asked_ref[0, t:t + 1, :] for t in range(lines)], axis=1)
        values = in_ref[...].reshape(slots, width)

        def step(t, carry):
            rows = lax.broadcasted_iota(I32, (tile, slots), 0) + t * tile
            hit = jnp.where(rows == line, 1.0, 0.0).astype(BF)
            out_ref[0, pl.ds(pl.multiple_of(t * tile, tile), tile), :] = mm(hit, values)
            return carry

        lax.fori_loop(0, rows_own // tile, step, 0)

    return pl.pallas_call(
        kernel,
        out_shape=jax.ShapeDtypeStruct((levels, rows_own, width), F32),
        grid=(levels,),
        in_specs=[
            pl.BlockSpec((1, lines, lane), lambda l: (l, 0, 0)),
            pl.BlockSpec((owners, cap, width), lambda l: (0, l, 0)),
        ],
        out_specs=pl.BlockSpec((1, rows_own, width), lambda l: (l, 0, 0)),
        name="collect",
    )(asked, incoming)


def turn(feats, place):
    items, depth = feats[0].shape
    ny = len(feats)
    hy = ny // 2
    cols = 256

    def kernel(place_ref, *refs):
        here_ref, there_ref = refs[ny:]
        for k in range(ny):
            spot = place_ref[k]
            flat = refs[k][...].T

            @pl.when(spot < hy)
            def _():
                here_ref[spot] = flat

            @pl.when(spot >= hy)
            def _():
                there_ref[spot - hy] = flat

    out = pl.BlockSpec((hy, cols, items), lambda i: (0, i, 0))
    return pl.pallas_call(
        kernel,
        out_shape=[jax.ShapeDtypeStruct((hy, depth, items), BF)] * 2,
        grid=(depth // cols,),
        in_specs=[SMEM] + [pl.BlockSpec((items, cols), lambda i: (0, i))] * ny,
        out_specs=[out] * 2,
        cost_estimate=pl.CostEstimate(flops=0, bytes_accessed=8 << 20, transcendentals=0),
        name="turn",
    )(place, *feats)


def back(grads, hidden, slope, w_out, feats_there, place, step):
    items, hid = hidden.shape
    ny, width = w_out.shape[:2]
    rows = feats_there.shape[0]

    def kernel(place_ref, *refs):
        g_refs, (hid_ref, slope_ref, wo_ref, f_ref, pre_ref, out_ref, there_ref) = refs[:ny], refs[ny:]
        acc = None
        for k in range(ny):
            part = mm(g_refs[k][...], wo_ref[place_ref[k]])
            acc = part if acc is None else acc + part
        pre_ref[...] = (acc * slope_ref[...]).astype(BF)

        def product(t, carry):
            cut = pl.ds(pl.multiple_of(t * 512, 512), 512)
            there_ref[cut, :] = mm(f_ref[cut, :], pre_ref[:, :step]).astype(BF)
            return carry

        lax.fori_loop(0, rows // 512, product, 0)
        for k in range(ny):
            out_ref[place_ref[k]] = mm(g_refs[k][...], hid_ref[...], ((0,), (0,)))

    return pl.pallas_call(
        kernel,
        out_shape=[
            jax.ShapeDtypeStruct((items, hid), BF),
            jax.ShapeDtypeStruct((ny, width, hid), F32),
            jax.ShapeDtypeStruct((rows, step), BF),
        ],
        in_specs=[SMEM] + [VMEM] * (ny + 4),
        out_specs=[VMEM] * 3,
        cost_estimate=pl.CostEstimate(flops=6 * items * hid * ny * width, bytes_accessed=6 << 20, transcendentals=0),
        name="back",
    )(place, *grads, hidden, slope, w_out, feats_there)


def cut_by_x(feats_t, pre, came, out_mine, out_came, order, nz, nx, c):
    items = feats_t.shape[2]
    hid = came.shape[1]
    in_rows = came.shape[0] // (nz * nx)
    hy = feats_t.shape[0]
    ny, width = out_mine.shape[:2]
    out_rows = hy * width // (nz * nx)
    both = in_rows + out_rows
    feats_t = feats_t.reshape(-1, items)
    out_mine = out_mine.reshape(ny * width, -1)
    out_came = out_came.reshape(ny * width, -1)
    group = 4
    many, few = group * nx * in_rows, group * nx * out_rows
    ahead = hy * width // few

    def kernel(order_ref, f_ref, p_ref, came_ref, om_ref, oc_ref, own_ref, *rest):
        sends, part = rest[:-1], rest[-1]
        total = (mm(f_ref[...], p_ref[...]) + came_ref[...].astype(F32)).reshape(group, nx, in_rows, hid)
        outs = (om_ref[...] + oc_ref[...]).reshape(group, nx, out_rows, hid)
        for g in range(group):
            part[:, :in_rows] = total[g]
            part[:, in_rows:] = outs[g]
            own_ref[g] = part[order_ref[0]]
            for k, send in enumerate(sends):
                send[g] = part[order_ref[k + 1]].astype(BF)

    block = pl.BlockSpec((group, both, hid), lambda t: (t, 0, 0))
    return pl.pallas_call(
        kernel,
        out_shape=[jax.ShapeDtypeStruct((nz, both, hid), F32)]
        + [jax.ShapeDtypeStruct((nz, both, hid), BF)] * (nx - 1),
        grid=(nz // group,),
        in_specs=[
            SMEM,
            pl.BlockSpec((many, items), lambda t: (t, 0)),
            pl.BlockSpec((items, hid), lambda t: (0, c)),
            pl.BlockSpec((many, hid), lambda t: (t, 0)),
            pl.BlockSpec((few, hid), lambda t: (t, c)),
            pl.BlockSpec((few, hid), lambda t: (ahead + t, c)),
        ],
        out_specs=[block] * nx,
        scratch_shapes=[pltpu.VMEM((nx, both, hid), F32)],
        cost_estimate=pl.CostEstimate(
            flops=2 * nz * nx * in_rows * items * hid, bytes_accessed=8 << 20, transcendentals=0),
        name="cut_by_x",
    )(order, feats_t, pre, came, out_mine, out_came)


def shards(features, w_in, w_out, codebook, codes, decoder_grad):
    s, x, y = lax.axis_index("s"), lax.axis_index("x"), lax.axis_index("y")
    ns, nz, nx, ny = (lax.axis_size(a) for a in ("s", "z", "x", "y"))
    owners = ns * nz * nx
    items, depth = features.shape
    levels, rows_own, width = codebook.shape
    cap = 2 * items // owners
    slots = owners * cap
    hid = w_in.shape[1]
    in_rows, out_rows = w_in.shape[0], w_out.shape[0]
    items_all = items * owners
    hy = ny // ns

    slot_all, payload = ask(codes, w_in, w_out, nz, nx, ns, rows_own, cap)
    got_z = exchange(payload, "z")
    w_z, digits = got_z[:, :in_rows + out_rows], got_z[:, in_rows + out_rows:, :slots // nz]
    feats = [features, shift(features, "y", 1), shift(features, "y", 2), shift(features, "y", -1)]
    hz = nz // 2
    from_left, from_right = shift(w_z, "x", 1), shift(w_z, "x", -1)
    near = [w_z, from_left, from_right, shift(from_left[:hz], "x", 1), shift(from_right[hz:], "x", -1)]
    spans = [(0, 0, 2), (1, 0, 2), (3, 0, 2), (2, 0, 1), (2, 1, 2)]
    other = [shift(block, "s", 1) for block in near]
    steps = jnp.arange(ny, dtype=I32)
    x_place = (x - steps) % nx
    y_place = (y - steps - hy * s) % ny
    y_send = (y + steps - hy * s) % ny
    x_send = (x + steps) % nx

    slot_list = [slot_all[l, :, 0] for l in range(levels)]
    slot_ids = jnp.arange(slots)
    digit_by = [
        digits, shift(digits, "x", 1), shift(digits, "x", 2), shift(digits, "x", -1)]
    none = jnp.zeros_like(digits)
    by_x = jnp.stack([
        sum(jnp.where((x - k) % nx == xa, digit_by[k], none) for k in range(nx)) for xa in range(nx)])
    far_x = shift(by_x, "s", 1)
    by_sx = jnp.stack([jnp.where(s == sa, by_x, far_x) for sa in range(ns)])
    mine = ((x * ns + s) * cap + jnp.arange(cap))[None, :] == jnp.arange(slots // nz)[:, None]
    picked = mm(by_sx.reshape(-1, slots // nz), mine.astype(BF)).reshape(ns, nx, nz, -1, cap)
    picked = jnp.transpose(picked, (3, 0, 2, 1, 4)).reshape(-1, slots).astype(jnp.int32)
    asked = (picked[0::2] * 32 + picked[1::2] - 1)[:levels].reshape(levels, -1, 128)
    chosen = pick(asked, codebook, owners)
    rows_back = exchange(chosen, OWN)
    words = [
        mm(
            (slot_list[l][:, None] == slot_ids[None, :]).astype(BF),
            rows_back[:, l * cap:(l + 1) * cap].reshape(slots, width),
        )
        for l in range(levels)
    ]

    hidden, slope, w_out_all, *lat = encode(
        feats, near, other, spans, jnp.concatenate([x_place, y_place, y_send]), in_rows, out_rows
    )
    far = shift(lat[2], "y", 2)
    fwd = shift(lat[1], "y", 1)
    bwd = shift(lat[3], "y", -1)
    feats_here, feats_there = turn(feats, y_place)
    words = lax.optimization_barrier(words)
    latent = lat[0] + fwd + bwd + far

    residual = latent
    pull_sum = jnp.zeros_like(latent)
    outgoing = []
    for l in range(levels):
        placed = mm((slot_ids[:, None] == slot_list[l][None, :]).astype(BF), residual.astype(BF))
        outgoing.append(placed.astype(BF).reshape(owners, cap, width))
        residual = residual - words[l]
        pull_sum = pull_sum + residual
    latent_grad = (
        (decoder_grad.astype(F32) + 2.0 * BETA * pull_sum) / jnp.sqrt(F32(items_all))
    ).astype(BF)
    grads = [latent_grad, shift(latent_grad, "y", 1), shift(latent_grad, "y", 2), shift(latent_grad, "y", -1)]
    incoming = exchange(jnp.concatenate(outgoing, axis=1), OWN)
    code_sums = collect(asked, incoming, rows_own)

    pieces = 2
    step = hid // pieces
    there_rows = feats_there.reshape(hy * depth, items)
    pre_grad, out_part, there_first = back(grads, hidden, slope, w_out_all, there_rows, y_place, step)
    out_came = shift(out_part, "s", 1)
    in_list, out_list = [], []
    for c in range(pieces):
        there = there_first if c == 0 else mm(there_rows, pre_grad[:, c * step:(c + 1) * step]).astype(BF)
        came = shift(there, "s", 1)
        own, to_1, to_2, to_3 = cut_by_x(feats_here, pre_grad, came, out_part, out_came, x_send, nz, nx, c)
        sum_x = (
            own
            + shift(to_1, "x", 1).astype(F32)
            + shift(to_2, "x", 2).astype(F32)
            + shift(to_3, "x", -1).astype(F32)
        ).astype(BF)
        over_z = exchange(sum_x, "z")
        in_list.append(jnp.sum(over_z[:, :in_rows].astype(F32), axis=0))
        out_list.append(jnp.sum(over_z[:, in_rows:].astype(F32), axis=0))
    return (jnp.concatenate(in_list, axis=1), jnp.concatenate(out_list, axis=1), code_sums)


def solution(mesh):
    fine = Mesh(mesh.devices.reshape(2, 8, 4, 4), ("s", "z", "x", "y"))
    in_specs = (
        P(OWN, "y"),
        P(OWN, "y"),
        P(OWN, "y"),
        P(None, OWN, "y"),
        P(None, OWN),
        P(OWN, "y"),
    )
    out_specs = (P(OWN, "y"), P(OWN, "y"), P(None, OWN, "y"))
    return jax.shard_map(shards, mesh=fine, in_specs=in_specs, out_specs=out_specs, check_vma=False)
```

```python
import jax
import jax.numpy as jnp
from jax import lax
from jax.experimental import pallas as pl
from jax.experimental.pallas import tpu as pltpu
from jax.sharding import Mesh, PartitionSpec as P

BETA = 0.25
BF = jnp.bfloat16
F32 = jnp.float32
I32 = jnp.int32
OWN = ("s", "z", "x")
VMEM = pl.BlockSpec(memory_space=pltpu.VMEM)
SMEM = pl.BlockSpec(memory_space=pltpu.SMEM)


def shift(value, axis, by):
    size = lax.axis_size(axis)
    return lax.ppermute(value, axis, [(i, (i + by) % size) for i in range(size)])


def exchange(value, axis):
    return lax.all_to_all(value, axis, split_axis=0, concat_axis=0, tiled=True)


def mm(a, b, dims=((1,), (0,))):
    return lax.dot_general(a, b, (dims, ((), ())), preferred_element_type=F32)


def split(value, size):
    if size & (size - 1) == 0:
        return lax.shift_right_logical(value, jnp.full_like(value, size.bit_length() - 1)), value & (size - 1)
    return value // size, value % size


def encode(feats, near, other, spans, place, in_rows, out_rows):
    items, depth = feats[0].shape
    nz, _, hid = near[0].shape
    many = len(near)
    nx = 1 + max(k for k, _, _ in spans)
    ny = len(feats)
    hz = nz * 2 // ny
    width = hz * nx * out_rows
    tile = items // 2

    def kernel(place_ref, *refs):
        f_refs, refs = refs[:ny], refs[ny:]
        n_refs, refs = refs[:many], refs[many:]
        o_refs, refs = refs[:many], refs[many:]
        hid_ref, slope_ref, wo_ref = refs[:3]
        lat_refs, (w_ref, wo32_ref) = refs[3:3 + ny], refs[3 + ny:]

        @pl.when(pl.program_id(0) == 0)
        def _():
            for (k, low, high), *pair in zip(spans, n_refs, o_refs):
                xk = place_ref[k]
                for r, ref in enumerate(pair):
                    for zh in range(low, high):
                        p = r * (ny // 2) + zh
                        cut = ref[(zh - low) * hz:(zh - low + 1) * hz]
                        w_ref[p, :, xk] = cut[:, :in_rows]
                        wo32_ref[p, :, xk] = cut[:, in_rows:].astype(F32)
            for p in range(ny):
                wo_ref[p] = wo32_ref[p].reshape(width, hid).astype(BF)

        acc = None
        for k in range(ny):
            part = mm(f_refs[k][...], w_ref[place_ref[nx + k]].reshape(depth, hid))
            acc = part if acc is None else acc + part
        logistic = jax.nn.sigmoid(acc)
        hidden = (acc * logistic).astype(BF)
        hid_ref[...] = hidden
        slope_ref[...] = logistic * (1.0 + acc * (1.0 - logistic))
        for j in range(ny):
            lat_refs[j][...] = mm(hidden, wo_ref[place_ref[nx + ny + j]], ((1,), (1,)))

    def rows(cols):
        return pl.BlockSpec((tile, cols), lambda t: (t, 0))

    return pl.pallas_call(
        kernel,
        out_shape=[
            jax.ShapeDtypeStruct((items, hid), BF),
            jax.ShapeDtypeStruct((items, hid), F32),
            jax.ShapeDtypeStruct((ny, width, hid), BF),
        ] + [jax.ShapeDtypeStruct((items, width), F32)] * ny,
        grid=(items // tile,),
        in_specs=[SMEM] + [rows(depth)] * ny + [VMEM] * (2 * many),
        out_specs=[rows(hid)] * 2 + [pl.BlockSpec((ny, width, hid), lambda t: (0, 0, 0))] + [rows(width)] * ny,
        scratch_shapes=[
            pltpu.VMEM((ny, hz, nx, in_rows, hid), BF),
            pltpu.VMEM((ny, hz, nx, out_rows, hid), F32),
        ],
        cost_estimate=pl.CostEstimate(
            flops=2 * items * hid * ny * (depth + width), bytes_accessed=12 << 20, transcendentals=items * hid),
        compiler_params=pltpu.CompilerParams(vmem_limit_bytes=48 << 20),
        name="encode",
    )(place, *feats, *near, *other)


def ask(codes, w_in, w_out, nz, nx, ns, rows_own, cap):
    levels, items = codes.shape
    in_rows, hid = w_in.shape
    out_rows = w_out.shape[0]
    owners = ns * nz * nx
    slots = owners * cap
    group = slots // nz
    digit_rows = 8
    lane = 128

    def kernel(codes_ref, wi_ref, wo_ref, slot_ref, pay_ref, col_ref, found_ref):
        fill = jnp.zeros((8 - levels, lane), I32)
        for t in range(items // lane):
            block = jnp.concatenate([codes_ref[:, t * lane:(t + 1) * lane], fill], axis=0).T
            for l in range(levels):
                col_ref[l, t * lane:(t + 1) * lane, :] = block[:, l:l + 1]
        found_ref[...] = jnp.zeros_like(found_ref)

        def level(l, carry):
            code_row, code_col = codes_ref[pl.ds(l, 1), :], col_ref[l]
            own_row, _ = split(code_row, rows_own)
            own_col, row_col = split(code_col, rows_own)
            first = lax.broadcasted_iota(I32, (items, items), 0)
            second = lax.broadcasted_iota(I32, (items, items), 1)
            before = jnp.where(second < first, jnp.where(own_col == own_row, 1.0, 0.0), 0.0)
            rank = jnp.sum(before, axis=1, keepdims=True).astype(I32)
            slot_ref[l] = own_col * cap + rank
            section, rest = split(own_col, nz * nx)
            spot = (rest * ns + section) * cap + rank
            value = (row_col + 1).astype(F32)
            lanes = lax.broadcasted_iota(I32, (items, slots), 1)
            want = jnp.sum(jnp.where(lanes == spot, value, 0.0), axis=0, keepdims=True).astype(I32)
            high, low = split(want, 32)
            found_ref[pl.ds(2 * l, 1), :] = high.astype(F32)
            found_ref[pl.ds(2 * l + 1, 1), :] = low.astype(F32)
            return carry

        lax.fori_loop(0, levels, level, 0)
        rest = jnp.zeros((digit_rows, hid - group), F32)
        for z in range(nz):
            pay_ref[z, :in_rows] = wi_ref[...]
            digits = jnp.concatenate([found_ref[:, z * group:(z + 1) * group], rest], axis=1)
            pay_ref[z, in_rows:] = jnp.concatenate([wo_ref[...].astype(F32), digits], axis=0).astype(BF)

    return pl.pallas_call(
        kernel,
        out_shape=[
            jax.ShapeDtypeStruct((levels, items, 1), I32),
            jax.ShapeDtypeStruct((nz, in_rows + out_rows + digit_rows, hid), BF),
        ],
        in_specs=[VMEM] * 3,
        out_specs=[VMEM] * 2,
        scratch_shapes=[pltpu.VMEM((levels, items, 1), I32), pltpu.VMEM((digit_rows, slots), F32)],
        name="ask",
    )(codes, w_in, w_out)


def pick(asked, book, owners):
    levels, lines, lane = asked.shape
    rows_own, width = book.shape[1:]
    slots = lines * lane
    cap = slots // owners
    tile = 256

    def kernel(asked_ref, book_ref, out_ref, col_ref):
        turned = asked_ref[0].T
        for t in range(lines):
            col_ref[t * lane:(t + 1) * lane, :] = turned[:, t:t + 1]

        def step(t, carry):
            col = col_ref[pl.ds(pl.multiple_of(t * tile, tile), tile), :]
            hit = jnp.where(lax.broadcasted_iota(I32, (tile, rows_own), 1) == col, 1.0, 0.0).astype(BF)
            got = mm(hit, book_ref[0]).astype(BF)
            out_ref[pl.ds(t * (tile // cap), tile // cap)] = got.reshape(tile // cap, cap, width)
            return carry

        lax.fori_loop(0, slots // tile, step, 0)

    return pl.pallas_call(
        kernel,
        out_shape=jax.ShapeDtypeStruct((owners, levels * cap, width), BF),
        grid=(levels,),
        in_specs=[
            pl.BlockSpec((1, lines, lane), lambda l: (l, 0, 0)),
            pl.BlockSpec((1, rows_own, width), lambda l: (l, 0, 0)),
        ],
        out_specs=pl.BlockSpec((owners, cap, width), lambda l: (0, l, 0)),
        scratch_shapes=[pltpu.VMEM((slots, 1), I32)],
        name="pick",
    )(asked, book)


def collect(asked, incoming, rows_own):
    levels, lines, lane = asked.shape
    owners, _, width = incoming.shape
    slots = lines * lane
    cap = slots // owners
    tile = 256

    def kernel(asked_ref, in_ref, out_ref):
        line = jnp.concatenate([asked_ref[0, t:t + 1, :] for t in range(lines)], axis=1)
        values = in_ref[...].reshape(slots, width)

        def step(t, carry):
            rows = lax.broadcasted_iota(I32, (tile, slots), 0) + t * tile
            hit = jnp.where(rows == line, 1.0, 0.0).astype(BF)
            out_ref[0, pl.ds(pl.multiple_of(t * tile, tile), tile), :] = mm(hit, values)
            return carry

        lax.fori_loop(0, rows_own // tile, step, 0)

    return pl.pallas_call(
        kernel,
        out_shape=jax.ShapeDtypeStruct((levels, rows_own, width), F32),
        grid=(levels,),
        in_specs=[
            pl.BlockSpec((1, lines, lane), lambda l: (l, 0, 0)),
            pl.BlockSpec((owners, cap, width), lambda l: (0, l, 0)),
        ],
        out_specs=pl.BlockSpec((1, rows_own, width), lambda l: (l, 0, 0)),
        compiler_params=pltpu.CompilerParams(vmem_limit_bytes=12 << 20),
        name="collect",
    )(asked, incoming)


def turn(feats, place):
    items, depth = feats[0].shape
    ny = len(feats)
    hy = ny // 2
    cols = 256

    def kernel(place_ref, *refs):
        here_ref, there_ref = refs[ny:]
        for k in range(ny):
            spot = place_ref[k]
            flat = refs[k][...].T

            @pl.when(spot < hy)
            def _():
                here_ref[spot] = flat

            @pl.when(spot >= hy)
            def _():
                there_ref[spot - hy] = flat

    out = pl.BlockSpec((hy, cols, items), lambda i: (0, i, 0))
    return pl.pallas_call(
        kernel,
        out_shape=[jax.ShapeDtypeStruct((hy, depth, items), BF)] * 2,
        grid=(depth // cols,),
        in_specs=[SMEM] + [pl.BlockSpec((items, cols), lambda i: (0, i))] * ny,
        out_specs=[out] * 2,
        cost_estimate=pl.CostEstimate(flops=0, bytes_accessed=8 << 20, transcendentals=0),
        name="turn",
    )(place, *feats)


def back(grads, hidden, slope, w_out, feats_there, place, step):
    items, hid = hidden.shape
    ny, width = w_out.shape[:2]
    rows = feats_there.shape[0]

    def kernel(place_ref, *refs):
        g_refs, (hid_ref, slope_ref, wo_ref, f_ref, pre_ref, out_ref, there_ref) = refs[:ny], refs[ny:]
        grads_all = jnp.concatenate([g_refs[k][...] for k in range(ny)], axis=1)
        w_all = jnp.concatenate([wo_ref[place_ref[k]] for k in range(ny)], axis=0)
        pre_ref[...] = (mm(grads_all, w_all) * slope_ref[...]).astype(BF)

        def product(t, carry):
            cut = pl.ds(pl.multiple_of(t * 512, 512), 512)
            there_ref[cut, :] = mm(f_ref[cut, :], pre_ref[:, :step]).astype(BF)
            return carry

        lax.fori_loop(0, rows // 512, product, 0)
        outs = mm(grads_all, hid_ref[...], ((0,), (0,)))
        for k in range(ny):
            out_ref[place_ref[k]] = outs[k * width:(k + 1) * width]

    return pl.pallas_call(
        kernel,
        out_shape=[
            jax.ShapeDtypeStruct((items, hid), BF),
            jax.ShapeDtypeStruct((ny, width, hid), F32),
            jax.ShapeDtypeStruct((rows, step), BF),
        ],
        in_specs=[SMEM] + [VMEM] * (ny + 4),
        out_specs=[VMEM] * 3,
        cost_estimate=pl.CostEstimate(flops=6 * items * hid * ny * width, bytes_accessed=6 << 20, transcendentals=0),
        name="back",
    )(place, *grads, hidden, slope, w_out, feats_there)


def cut_by_x(feats_t, pre, came, out_mine, out_came, order, nz, nx, c):
    items = feats_t.shape[2]
    hid = came.shape[1]
    in_rows = came.shape[0] // (nz * nx)
    hy = feats_t.shape[0]
    ny, width = out_mine.shape[:2]
    out_rows = hy * width // (nz * nx)
    both = in_rows + out_rows
    feats_t = feats_t.reshape(-1, items)
    out_mine = out_mine.reshape(ny * width, -1)
    out_came = out_came.reshape(ny * width, -1)
    group = 4
    many, few = group * nx * in_rows, group * nx * out_rows
    ahead = hy * width // few

    def kernel(order_ref, f_ref, p_ref, came_ref, om_ref, oc_ref, own_ref, *rest):
        sends, part = rest[:-1], rest[-1]
        total = (mm(f_ref[...], p_ref[...]) + came_ref[...].astype(F32)).reshape(group, nx, in_rows, hid)
        outs = (om_ref[...] + oc_ref[...]).reshape(group, nx, out_rows, hid)
        for g in range(group):
            part[:, :in_rows] = total[g]
            part[:, in_rows:] = outs[g]
            own_ref[g] = part[order_ref[0]]
            for k, send in enumerate(sends):
                send[g] = part[order_ref[k + 1]].astype(BF)

    block = pl.BlockSpec((group, both, hid), lambda t: (t, 0, 0))
    return pl.pallas_call(
        kernel,
        out_shape=[jax.ShapeDtypeStruct((nz, both, hid), F32)]
        + [jax.ShapeDtypeStruct((nz, both, hid), BF)] * (nx - 1),
        grid=(nz // group,),
        in_specs=[
            SMEM,
            pl.BlockSpec((many, items), lambda t: (t, 0)),
            pl.BlockSpec((items, hid), lambda t: (0, c)),
            pl.BlockSpec((many, hid), lambda t: (t, 0)),
            pl.BlockSpec((few, hid), lambda t: (t, c)),
            pl.BlockSpec((few, hid), lambda t: (ahead + t, c)),
        ],
        out_specs=[block] * nx,
        scratch_shapes=[pltpu.VMEM((nx, both, hid), F32)],
        cost_estimate=pl.CostEstimate(
            flops=2 * nz * nx * in_rows * items * hid, bytes_accessed=8 << 20, transcendentals=0),
        compiler_params=pltpu.CompilerParams(vmem_limit_bytes=16 << 20),
        name="cut_by_x",
    )(order, feats_t, pre, came, out_mine, out_came)


def shards(features, w_in, w_out, codebook, codes, decoder_grad):
    s, x, y = lax.axis_index("s"), lax.axis_index("x"), lax.axis_index("y")
    ns, nz, nx, ny = (lax.axis_size(a) for a in ("s", "z", "x", "y"))
    owners = ns * nz * nx
    items, depth = features.shape
    levels, rows_own, width = codebook.shape
    cap = 2 * items // owners
    slots = owners * cap
    hid = w_in.shape[1]
    in_rows, out_rows = w_in.shape[0], w_out.shape[0]
    items_all = items * owners
    hy = ny // ns

    slot_all, payload = ask(codes, w_in, w_out, nz, nx, ns, rows_own, cap)
    got_z = exchange(payload, "z")
    w_z, digits = got_z[:, :in_rows + out_rows], got_z[:, in_rows + out_rows:, :slots // nz]
    feats = [features, shift(features, "y", 1), shift(features, "y", 2), shift(features, "y", -1)]
    hz = nz // 2
    from_left, from_right = shift(w_z, "x", 1), shift(w_z, "x", -1)
    near = [w_z, from_left, from_right, shift(from_left[:hz], "x", 1), shift(from_right[hz:], "x", -1)]
    spans = [(0, 0, 2), (1, 0, 2), (3, 0, 2), (2, 0, 1), (2, 1, 2)]
    other = [shift(block, "s", 1) for block in near]
    steps = jnp.arange(ny, dtype=I32)
    x_place = (x - steps) % nx
    y_place = (y - steps - hy * s) % ny
    y_send = (y + steps - hy * s) % ny
    x_send = (x + steps) % nx

    slot_list = [slot_all[l, :, 0] for l in range(levels)]
    slot_ids = jnp.arange(slots)
    digit_by = [
        digits, shift(digits, "x", 1), shift(digits, "x", 2), shift(digits, "x", -1)]
    none = jnp.zeros_like(digits)
    by_x = jnp.stack([
        sum(jnp.where((x - k) % nx == xa, digit_by[k], none) for k in range(nx)) for xa in range(nx)])
    far_x = shift(by_x, "s", 1)
    by_sx = jnp.stack([jnp.where(s == sa, by_x, far_x) for sa in range(ns)])
    mine = ((x * ns + s) * cap + jnp.arange(cap))[None, :] == jnp.arange(slots // nz)[:, None]
    picked = mm(by_sx.reshape(-1, slots // nz), mine.astype(BF)).reshape(ns, nx, nz, -1, cap)
    picked = jnp.transpose(picked, (3, 0, 2, 1, 4)).reshape(-1, slots).astype(jnp.int32)
    asked = (picked[0::2] * 32 + picked[1::2] - 1)[:levels].reshape(levels, -1, 128)
    chosen = pick(asked, codebook, owners)
    rows_back = exchange(chosen, OWN)
    words = [
        mm(
            (slot_list[l][:, None] == slot_ids[None, :]).astype(BF),
            rows_back[:, l * cap:(l + 1) * cap].reshape(slots, width),
        )
        for l in range(levels)
    ]

    hidden, slope, w_out_all, *lat = encode(
        feats, near, other, spans, jnp.concatenate([x_place, y_place, y_send]), in_rows, out_rows
    )
    far = shift(lat[2], "y", 2)
    fwd = shift(lat[1], "y", 1)
    bwd = shift(lat[3], "y", -1)
    feats_here, feats_there = turn(feats, y_place)
    words = lax.optimization_barrier(words)
    latent = lat[0] + fwd + bwd + far

    residual = latent
    pull_sum = jnp.zeros_like(latent)
    outgoing = []
    for l in range(levels):
        placed = mm((slot_ids[:, None] == slot_list[l][None, :]).astype(BF), residual.astype(BF))
        outgoing.append(placed.astype(BF).reshape(owners, cap, width))
        residual = residual - words[l]
        pull_sum = pull_sum + residual
    latent_grad = (
        (decoder_grad.astype(F32) + 2.0 * BETA * pull_sum) / jnp.sqrt(F32(items_all))
    ).astype(BF)
    grads = [latent_grad, shift(latent_grad, "y", 1), shift(latent_grad, "y", 2), shift(latent_grad, "y", -1)]
    incoming = exchange(jnp.concatenate(outgoing, axis=1), OWN)
    code_sums = collect(asked, incoming, rows_own)

    pieces = 2
    step = hid // pieces
    there_rows = feats_there.reshape(hy * depth, items)
    pre_grad, out_part, there_first = back(grads, hidden, slope, w_out_all, there_rows, y_place, step)
    out_came = shift(out_part, "s", 1)
    in_list, out_list = [], []
    for c in range(pieces):
        there = there_first if c == 0 else mm(there_rows, pre_grad[:, c * step:(c + 1) * step]).astype(BF)
        came = shift(there, "s", 1)
        own, to_1, to_2, to_3 = cut_by_x(feats_here, pre_grad, came, out_part, out_came, x_send, nz, nx, c)
        sum_x = (
            own
            + shift(to_1, "x", 1).astype(F32)
            + shift(to_2, "x", 2).astype(F32)
            + shift(to_3, "x", -1).astype(F32)
        ).astype(BF)
        over_z = exchange(sum_x, "z")
        in_list.append(jnp.sum(over_z[:, :in_rows].astype(F32), axis=0))
        out_list.append(jnp.sum(over_z[:, in_rows:].astype(F32), axis=0))
    return (jnp.concatenate(in_list, axis=1), jnp.concatenate(out_list, axis=1), code_sums)


def solution(mesh):
    fine = Mesh(mesh.devices.reshape(2, 8, 4, 4), ("s", "z", "x", "y"))
    in_specs = (
        P(OWN, "y"),
        P(OWN, "y"),
        P(OWN, "y"),
        P(None, OWN, "y"),
        P(None, OWN),
        P(OWN, "y"),
    )
    out_specs = (P(OWN, "y"), P(OWN, "y"), P(None, OWN, "y"))
    return jax.shard_map(shards, mesh=fine, in_specs=in_specs, out_specs=out_specs, check_vma=False)
```

```python
import jax
import jax.numpy as jnp
from jax import lax
from jax.experimental import pallas as pl
from jax.experimental.pallas import tpu as pltpu
from jax.sharding import Mesh, PartitionSpec as P

BETA = 0.25
BF = jnp.bfloat16
F32 = jnp.float32
I32 = jnp.int32
OWN = ("s", "z", "x")
VMEM = pl.BlockSpec(memory_space=pltpu.VMEM)
SMEM = pl.BlockSpec(memory_space=pltpu.SMEM)
HBM = pl.BlockSpec(memory_space=pltpu.HBM)


def shift(value, axis, by):
    size = lax.axis_size(axis)
    return lax.ppermute(value, axis, [(i, (i + by) % size) for i in range(size)])


def exchange(value, axis):
    return lax.all_to_all(value, axis, split_axis=0, concat_axis=0, tiled=True)


def mm(a, b, dims=((1,), (0,))):
    return lax.dot_general(a, b, (dims, ((), ())), preferred_element_type=F32)


def split(value, size):
    if size & (size - 1) == 0:
        return lax.shift_right_logical(value, jnp.full_like(value, size.bit_length() - 1)), value & (size - 1)
    return value // size, value % size


def encode(feats, near, other, spans, place, in_rows, out_rows):
    items, depth = feats[0].shape
    nz, _, hid = near[0].shape
    many = len(near)
    nx = 1 + max(k for k, _, _ in spans)
    ny = len(feats)
    hz = nz * 2 // ny
    width = hz * nx * out_rows
    tile = items // 2

    def kernel(place_ref, *refs):
        f_refs, refs = refs[:ny], refs[ny:]
        n_refs, refs = refs[:many], refs[many:]
        o_refs, refs = refs[:many], refs[many:]
        hid_out, slope_ref, wo_out = refs[:3]
        lat_refs, (w_ref, wo32_ref, wo_ref, hid_ref, wo_sem, hid_sem) = refs[3:3 + ny], refs[3 + ny:]
        t = pl.program_id(0)

        def send_wo():
            return pltpu.make_async_copy(wo_ref, wo_out, wo_sem)

        def send_hidden(i):
            rows_to = hid_out.at[pl.ds(pl.multiple_of(i * tile, tile), tile)]
            return pltpu.make_async_copy(hid_ref.at[i], rows_to, hid_sem.at[i])

        @pl.when(pl.program_id(0) == 0)
        def _():
            for (k, low, high), *pair in zip(spans, n_refs, o_refs):
                xk = place_ref[k]
                for r, ref in enumerate(pair):
                    for zh in range(low, high):
                        p = r * (ny // 2) + zh
                        cut = ref[(zh - low) * hz:(zh - low + 1) * hz]
                        w_ref[p, :, xk] = cut[:, :in_rows]
                        wo32_ref[p, :, xk] = cut[:, in_rows:].astype(F32)
            for p in range(ny):
                wo_ref[p] = wo32_ref[p].reshape(width, hid).astype(BF)
            send_wo().start()

        acc = None
        for k in range(ny):
            part = mm(f_refs[k][...], w_ref[place_ref[nx + k]].reshape(depth, hid))
            acc = part if acc is None else acc + part
        logistic = jax.nn.sigmoid(acc)
        hidden = (acc * logistic).astype(BF)
        hid_ref[t] = hidden
        send_hidden(t).start()
        slope_ref[...] = logistic * (1.0 + acc * (1.0 - logistic))
        for j in range(ny):
            lat_refs[j][...] = mm(hidden, wo_ref[place_ref[nx + ny + j]], ((1,), (1,)))

        @pl.when(t == items // tile - 1)
        def _():
            send_wo().wait()
            for i in range(items // tile):
                send_hidden(i).wait()

    def rows(cols):
        return pl.BlockSpec((tile, cols), lambda t: (t, 0))

    return pl.pallas_call(
        kernel,
        out_shape=[
            pltpu.HBM((items, hid), BF),
            jax.ShapeDtypeStruct((items, hid), F32),
            pltpu.HBM((ny, width, hid), BF),
        ] + [jax.ShapeDtypeStruct((items, width), F32)] * ny,
        grid=(items // tile,),
        in_specs=[SMEM] + [rows(depth)] * ny + [VMEM] * (2 * many),
        out_specs=[HBM, rows(hid), HBM] + [rows(width)] * ny,
        scratch_shapes=[
            pltpu.VMEM((ny, hz, nx, in_rows, hid), BF),
            pltpu.VMEM((ny, hz, nx, out_rows, hid), F32),
            pltpu.VMEM((ny, width, hid), BF),
            pltpu.VMEM((items // tile, tile, hid), BF),
            pltpu.SemaphoreType.DMA,
            pltpu.SemaphoreType.DMA((items // tile,)),
        ],
        cost_estimate=pl.CostEstimate(
            flops=2 * items * hid * ny * (depth + width), bytes_accessed=12 << 20, transcendentals=items * hid),
        compiler_params=pltpu.CompilerParams(vmem_limit_bytes=48 << 20),
        name="encode",
    )(place, *feats, *near, *other)


def ask(codes, w_in, w_out, nz, nx, ns, rows_own, cap):
    levels, items = codes.shape
    in_rows, hid = w_in.shape
    out_rows = w_out.shape[0]
    owners = ns * nz * nx
    slots = owners * cap
    group = slots // nz
    digit_rows = 8
    lane = 128

    def kernel(codes_ref, wi_ref, wo_ref, slot_ref, pay_ref, col_ref, found_ref):
        fill = jnp.zeros((8 - levels, lane), I32)
        for t in range(items // lane):
            block = jnp.concatenate([codes_ref[:, t * lane:(t + 1) * lane], fill], axis=0).T
            for l in range(levels):
                col_ref[l, t * lane:(t + 1) * lane, :] = block[:, l:l + 1]
        found_ref[...] = jnp.zeros_like(found_ref)

        def level(l, carry):
            code_row, code_col = codes_ref[pl.ds(l, 1), :], col_ref[l]
            own_row, _ = split(code_row, rows_own)
            own_col, row_col = split(code_col, rows_own)
            first = lax.broadcasted_iota(I32, (items, items), 0)
            second = lax.broadcasted_iota(I32, (items, items), 1)
            before = jnp.where(second < first, jnp.where(own_col == own_row, 1.0, 0.0), 0.0)
            rank = jnp.sum(before, axis=1, keepdims=True).astype(I32)
            slot_ref[l] = own_col * cap + rank
            section, rest = split(own_col, nz * nx)
            spot = (rest * ns + section) * cap + rank
            value = (row_col + 1).astype(F32)
            lanes = lax.broadcasted_iota(I32, (items, slots), 1)
            want = jnp.sum(jnp.where(lanes == spot, value, 0.0), axis=0, keepdims=True).astype(I32)
            high, low = split(want, 32)
            found_ref[pl.ds(2 * l, 1), :] = high.astype(F32)
            found_ref[pl.ds(2 * l + 1, 1), :] = low.astype(F32)
            return carry

        lax.fori_loop(0, levels, level, 0)
        rest = jnp.zeros((digit_rows, hid - group), F32)
        for z in range(nz):
            pay_ref[z, :in_rows] = wi_ref[...]
            digits = jnp.concatenate([found_ref[:, z * group:(z + 1) * group], rest], axis=1)
            pay_ref[z, in_rows:] = jnp.concatenate([wo_ref[...].astype(F32), digits], axis=0).astype(BF)

    return pl.pallas_call(
        kernel,
        out_shape=[
            jax.ShapeDtypeStruct((levels, items, 1), I32),
            jax.ShapeDtypeStruct((nz, in_rows + out_rows + digit_rows, hid), BF),
        ],
        in_specs=[VMEM] * 3,
        out_specs=[VMEM] * 2,
        scratch_shapes=[pltpu.VMEM((levels, items, 1), I32), pltpu.VMEM((digit_rows, slots), F32)],
        name="ask",
    )(codes, w_in, w_out)


def pick(asked, book, owners):
    levels, lines, lane = asked.shape
    rows_own, width = book.shape[1:]
    slots = lines * lane
    cap = slots // owners
    tile = 256

    def kernel(asked_ref, book_ref, out_ref, col_ref):
        turned = asked_ref[0].T
        for t in range(lines):
            col_ref[t * lane:(t + 1) * lane, :] = turned[:, t:t + 1]

        def step(t, carry):
            col = col_ref[pl.ds(pl.multiple_of(t * tile, tile), tile), :]
            hit = jnp.where(lax.broadcasted_iota(I32, (tile, rows_own), 1) == col, 1.0, 0.0).astype(BF)
            got = mm(hit, book_ref[0]).astype(BF)
            out_ref[pl.ds(t * (tile // cap), tile // cap)] = got.reshape(tile // cap, cap, width)
            return carry

        lax.fori_loop(0, slots // tile, step, 0)

    return pl.pallas_call(
        kernel,
        out_shape=jax.ShapeDtypeStruct((owners, levels * cap, width), BF),
        grid=(levels,),
        in_specs=[
            pl.BlockSpec((1, lines, lane), lambda l: (l, 0, 0)),
            pl.BlockSpec((1, rows_own, width), lambda l: (l, 0, 0)),
        ],
        out_specs=pl.BlockSpec((owners, cap, width), lambda l: (0, l, 0)),
        scratch_shapes=[pltpu.VMEM((slots, 1), I32)],
        name="pick",
    )(asked, book)


def collect(asked, incoming, rows_own):
    levels, lines, lane = asked.shape
    owners, _, width = incoming.shape
    slots = lines * lane
    cap = slots // owners
    tile = 256

    def kernel(asked_ref, in_ref, out_ref):
        line = jnp.concatenate([asked_ref[0, t:t + 1, :] for t in range(lines)], axis=1)
        values = in_ref[...].reshape(slots, width)

        def step(t, carry):
            rows = lax.broadcasted_iota(I32, (tile, slots), 0) + t * tile
            hit = jnp.where(rows == line, 1.0, 0.0).astype(BF)
            out_ref[0, pl.ds(pl.multiple_of(t * tile, tile), tile), :] = mm(hit, values)
            return carry

        lax.fori_loop(0, rows_own // tile, step, 0)

    return pl.pallas_call(
        kernel,
        out_shape=jax.ShapeDtypeStruct((levels, rows_own, width), F32),
        grid=(levels,),
        in_specs=[
            pl.BlockSpec((1, lines, lane), lambda l: (l, 0, 0)),
            pl.BlockSpec((owners, cap, width), lambda l: (0, l, 0)),
        ],
        out_specs=pl.BlockSpec((1, rows_own, width), lambda l: (l, 0, 0)),
        compiler_params=pltpu.CompilerParams(vmem_limit_bytes=12 << 20),
        name="collect",
    )(asked, incoming)


def turn(feats, place):
    items, depth = feats[0].shape
    ny = len(feats)
    hy = ny // 2
    cols = 256

    def kernel(place_ref, *refs):
        here_ref, there_ref = refs[ny:]
        for k in range(ny):
            spot = place_ref[k]
            flat = refs[k][...].T

            @pl.when(spot < hy)
            def _():
                here_ref[spot] = flat

            @pl.when(spot >= hy)
            def _():
                there_ref[spot - hy] = flat

    out = pl.BlockSpec((hy, cols, items), lambda i: (0, i, 0))
    return pl.pallas_call(
        kernel,
        out_shape=[jax.ShapeDtypeStruct((hy, depth, items), BF)] * 2,
        grid=(depth // cols,),
        in_specs=[SMEM] + [pl.BlockSpec((items, cols), lambda i: (0, i))] * ny,
        out_specs=[out] * 2,
        cost_estimate=pl.CostEstimate(flops=0, bytes_accessed=8 << 20, transcendentals=0),
        name="turn",
    )(place, *feats)


def back(grads, hidden, slope, w_out, feats_there, place, step):
    items, hid = hidden.shape
    ny, width = w_out.shape[:2]
    rows = feats_there.shape[0]

    def kernel(place_ref, *refs):
        g_refs, (hid_ref, slope_ref, wo_ref, f_ref, pre_ref, out_ref, there_ref) = refs[:ny], refs[ny:]
        grads_all = jnp.concatenate([g_refs[k][...] for k in range(ny)], axis=1)
        w_all = jnp.concatenate([wo_ref[place_ref[k]] for k in range(ny)], axis=0)
        pre_ref[...] = (mm(grads_all, w_all) * slope_ref[...]).astype(BF)

        def product(t, carry):
            cut = pl.ds(pl.multiple_of(t * 512, 512), 512)
            there_ref[cut, :] = mm(f_ref[cut, :], pre_ref[:, :step]).astype(BF)
            return carry

        lax.fori_loop(0, rows // 512, product, 0)
        outs = mm(grads_all, hid_ref[...], ((0,), (0,)))
        for k in range(ny):
            out_ref[place_ref[k]] = outs[k * width:(k + 1) * width]

    return pl.pallas_call(
        kernel,
        out_shape=[
            jax.ShapeDtypeStruct((items, hid), BF),
            jax.ShapeDtypeStruct((ny, width, hid), F32),
            jax.ShapeDtypeStruct((rows, step), BF),
        ],
        in_specs=[SMEM] + [VMEM] * (ny + 4),
        out_specs=[VMEM] * 3,
        cost_estimate=pl.CostEstimate(flops=6 * items * hid * ny * width, bytes_accessed=6 << 20, transcendentals=0),
        name="back",
    )(place, *grads, hidden, slope, w_out, feats_there)


def cut_by_x(feats_t, pre, came, out_mine, out_came, order, nz, nx, c):
    items = feats_t.shape[2]
    hid = came.shape[1]
    in_rows = came.shape[0] // (nz * nx)
    hy = feats_t.shape[0]
    ny, width = out_mine.shape[:2]
    out_rows = hy * width // (nz * nx)
    both = in_rows + out_rows
    feats_t = feats_t.reshape(-1, items)
    out_mine = out_mine.reshape(ny * width, -1)
    out_came = out_came.reshape(ny * width, -1)
    group = 4
    many, few = group * nx * in_rows, group * nx * out_rows
    ahead = hy * width // few

    def kernel(order_ref, f_ref, p_ref, came_ref, om_ref, oc_ref, own_ref, *rest):
        sends, part = rest[:-1], rest[-1]
        total = (mm(f_ref[...], p_ref[...]) + came_ref[...].astype(F32)).reshape(group, nx, in_rows, hid)
        outs = (om_ref[...] + oc_ref[...]).reshape(group, nx, out_rows, hid)
        for g in range(group):
            part[:, :in_rows] = total[g]
            part[:, in_rows:] = outs[g]
            own_ref[g] = part[order_ref[0]]
            for k, send in enumerate(sends):
                send[g] = part[order_ref[k + 1]].astype(BF)

    block = pl.BlockSpec((group, both, hid), lambda t: (t, 0, 0))
    return pl.pallas_call(
        kernel,
        out_shape=[jax.ShapeDtypeStruct((nz, both, hid), F32)]
        + [jax.ShapeDtypeStruct((nz, both, hid), BF)] * (nx - 1),
        grid=(nz // group,),
        in_specs=[
            SMEM,
            pl.BlockSpec((many, items), lambda t: (t, 0)),
            pl.BlockSpec((items, hid), lambda t: (0, c)),
            pl.BlockSpec((many, hid), lambda t: (t, 0)),
            pl.BlockSpec((few, hid), lambda t: (t, c)),
            pl.BlockSpec((few, hid), lambda t: (ahead + t, c)),
        ],
        out_specs=[block] * nx,
        scratch_shapes=[pltpu.VMEM((nx, both, hid), F32)],
        cost_estimate=pl.CostEstimate(
            flops=2 * nz * nx * in_rows * items * hid, bytes_accessed=8 << 20, transcendentals=0),
        compiler_params=pltpu.CompilerParams(vmem_limit_bytes=16 << 20),
        name="cut_by_x",
    )(order, feats_t, pre, came, out_mine, out_came)


def shards(features, w_in, w_out, codebook, codes, decoder_grad):
    s, x, y = lax.axis_index("s"), lax.axis_index("x"), lax.axis_index("y")
    ns, nz, nx, ny = (lax.axis_size(a) for a in ("s", "z", "x", "y"))
    owners = ns * nz * nx
    items, depth = features.shape
    levels, rows_own, width = codebook.shape
    cap = 2 * items // owners
    slots = owners * cap
    hid = w_in.shape[1]
    in_rows, out_rows = w_in.shape[0], w_out.shape[0]
    items_all = items * owners
    hy = ny // ns

    slot_all, payload = ask(codes, w_in, w_out, nz, nx, ns, rows_own, cap)
    got_z = exchange(payload, "z")
    w_z, digits = got_z[:, :in_rows + out_rows], got_z[:, in_rows + out_rows:, :slots // nz]
    feats = [features, shift(features, "y", 1), shift(features, "y", 2), shift(features, "y", -1)]
    hz = nz // 2
    from_left, from_right = shift(w_z, "x", 1), shift(w_z, "x", -1)
    near = [w_z, from_left, from_right, shift(from_left[:hz], "x", 1), shift(from_right[hz:], "x", -1)]
    spans = [(0, 0, 2), (1, 0, 2), (3, 0, 2), (2, 0, 1), (2, 1, 2)]
    other = [shift(block, "s", 1) for block in near]
    steps = jnp.arange(ny, dtype=I32)
    x_place = (x - steps) % nx
    y_place = (y - steps - hy * s) % ny
    y_send = (y + steps - hy * s) % ny
    x_send = (x + steps) % nx

    slot_list = [slot_all[l, :, 0] for l in range(levels)]
    slot_ids = jnp.arange(slots)
    digit_by = [
        digits, shift(digits, "x", 1), shift(digits, "x", 2), shift(digits, "x", -1)]
    none = jnp.zeros_like(digits)
    by_x = jnp.stack([
        sum(jnp.where((x - k) % nx == xa, digit_by[k], none) for k in range(nx)) for xa in range(nx)])
    far_x = shift(by_x, "s", 1)
    by_sx = jnp.stack([jnp.where(s == sa, by_x, far_x) for sa in range(ns)])
    mine = ((x * ns + s) * cap + jnp.arange(cap))[None, :] == jnp.arange(slots // nz)[:, None]
    picked = mm(by_sx.reshape(-1, slots // nz), mine.astype(BF)).reshape(ns, nx, nz, -1, cap)
    picked = jnp.transpose(picked, (3, 0, 2, 1, 4)).reshape(-1, slots).astype(jnp.int32)
    asked = (picked[0::2] * 32 + picked[1::2] - 1)[:levels].reshape(levels, -1, 128)
    chosen = pick(asked, codebook, owners)
    rows_back = exchange(chosen, OWN)
    words = [
        mm(
            (slot_list[l][:, None] == slot_ids[None, :]).astype(BF),
            rows_back[:, l * cap:(l + 1) * cap].reshape(slots, width),
        )
        for l in range(levels)
    ]

    hidden, slope, w_out_all, *lat = encode(
        feats, near, other, spans, jnp.concatenate([x_place, y_place, y_send]), in_rows, out_rows
    )
    far = shift(lat[2], "y", 2)
    fwd = shift(lat[1], "y", 1)
    bwd = shift(lat[3], "y", -1)
    feats_here, feats_there = turn(feats, y_place)
    words = lax.optimization_barrier(words)
    latent = lat[0] + fwd + bwd + far

    residual = latent
    pull_sum = jnp.zeros_like(latent)
    outgoing = []
    for l in range(levels):
        placed = mm((slot_ids[:, None] == slot_list[l][None, :]).astype(BF), residual.astype(BF))
        outgoing.append(placed.astype(BF).reshape(owners, cap, width))
        residual = residual - words[l]
        pull_sum = pull_sum + residual
    latent_grad = (
        (decoder_grad.astype(F32) + 2.0 * BETA * pull_sum) / jnp.sqrt(F32(items_all))
    ).astype(BF)
    grads = [latent_grad, shift(latent_grad, "y", 1), shift(latent_grad, "y", 2), shift(latent_grad, "y", -1)]
    incoming = exchange(jnp.concatenate(outgoing, axis=1), OWN)
    code_sums = collect(asked, incoming, rows_own)

    pieces = 2
    step = hid // pieces
    there_rows = feats_there.reshape(hy * depth, items)
    pre_grad, out_part, there_first = back(grads, hidden, slope, w_out_all, there_rows, y_place, step)
    out_came = shift(out_part, "s", 1)
    in_list, out_list = [], []
    for c in range(pieces):
        there = there_first if c == 0 else mm(there_rows, pre_grad[:, c * step:(c + 1) * step]).astype(BF)
        came = shift(there, "s", 1)
        own, to_1, to_2, to_3 = cut_by_x(feats_here, pre_grad, came, out_part, out_came, x_send, nz, nx, c)
        sum_x = (
            own
            + shift(to_1, "x", 1).astype(F32)
            + shift(to_2, "x", 2).astype(F32)
            + shift(to_3, "x", -1).astype(F32)
        ).astype(BF)
        over_z = exchange(sum_x, "z")
        in_list.append(jnp.sum(over_z[:, :in_rows].astype(F32), axis=0))
        out_list.append(jnp.sum(over_z[:, in_rows:].astype(F32), axis=0))
    return (jnp.concatenate(in_list, axis=1), jnp.concatenate(out_list, axis=1), code_sums)


def solution(mesh):
    fine = Mesh(mesh.devices.reshape(2, 8, 4, 4), ("s", "z", "x", "y"))
    in_specs = (
        P(OWN, "y"),
        P(OWN, "y"),
        P(OWN, "y"),
        P(None, OWN, "y"),
        P(None, OWN),
        P(OWN, "y"),
    )
    out_specs = (P(OWN, "y"), P(OWN, "y"), P(None, OWN, "y"))
    return jax.shard_map(shards, mesh=fine, in_specs=in_specs, out_specs=out_specs, check_vma=False)
```

```python
import jax
import jax.numpy as jnp
from jax import lax
from jax.experimental import pallas as pl
from jax.experimental.pallas import tpu as pltpu
from jax.sharding import Mesh, PartitionSpec as P

BETA = 0.25
BF = jnp.bfloat16
F32 = jnp.float32
I32 = jnp.int32
OWN = ("s", "z", "x")
VMEM = pl.BlockSpec(memory_space=pltpu.VMEM)
SMEM = pl.BlockSpec(memory_space=pltpu.SMEM)
HBM = pl.BlockSpec(memory_space=pltpu.HBM)


def shift(value, axis, by):
    size = lax.axis_size(axis)
    return lax.ppermute(value, axis, [(i, (i + by) % size) for i in range(size)])


def exchange(value, axis):
    return lax.all_to_all(value, axis, split_axis=0, concat_axis=0, tiled=True)


def mm(a, b, dims=((1,), (0,))):
    return lax.dot_general(a, b, (dims, ((), ())), preferred_element_type=F32)


def split(value, size):
    if size & (size - 1) == 0:
        return lax.shift_right_logical(value, jnp.full_like(value, size.bit_length() - 1)), value & (size - 1)
    return value // size, value % size


def encode(feats, near, other, spans, place, in_rows, out_rows):
    items, depth = feats[0].shape
    nz, _, hid = near[0].shape
    many = len(near)
    nx = 1 + max(k for k, _, _ in spans)
    ny = len(feats)
    hz = nz * 2 // ny
    width = hz * nx * out_rows
    tile = items // 2

    def kernel(place_ref, *refs):
        f_refs, refs = refs[:ny], refs[ny:]
        n_refs, refs = refs[:many], refs[many:]
        o_refs, refs = refs[:many], refs[many:]
        hid_out, slope_ref, wo_out = refs[:3]
        lat_refs, (w_ref, wo32_ref, wo_ref, hid_ref, wo_sem, hid_sem) = refs[3:3 + ny], refs[3 + ny:]
        t = pl.program_id(0)

        def send_wo():
            return pltpu.make_async_copy(wo_ref, wo_out, wo_sem)

        def send_hidden(i):
            rows_to = hid_out.at[pl.ds(pl.multiple_of(i * tile, tile), tile)]
            return pltpu.make_async_copy(hid_ref.at[i], rows_to, hid_sem.at[i])

        @pl.when(pl.program_id(0) == 0)
        def _():
            for (k, low, high), *pair in zip(spans, n_refs, o_refs):
                xk = place_ref[k]
                for r, ref in enumerate(pair):
                    for zh in range(low, high):
                        p = r * (ny // 2) + zh
                        cut = ref[(zh - low) * hz:(zh - low + 1) * hz]
                        w_ref[p, :, xk] = cut[:, :in_rows]
                        wo32_ref[p, :, xk] = cut[:, in_rows:].astype(F32)
            for p in range(ny):
                wo_ref[p] = wo32_ref[p].reshape(width, hid).astype(BF)
            send_wo().start()

        acc = None
        for k in range(ny):
            part = mm(f_refs[k][...], w_ref[place_ref[nx + k]].reshape(depth, hid))
            acc = part if acc is None else acc + part
        logistic = jax.nn.sigmoid(acc)
        hidden = (acc * logistic).astype(BF)
        hid_ref[t] = hidden
        send_hidden(t).start()
        slope_ref[...] = logistic * (1.0 + acc * (1.0 - logistic))
        for j in range(ny):
            lat_refs[j][...] = mm(hidden, wo_ref[place_ref[nx + ny + j]], ((1,), (1,)))

        @pl.when(t == items // tile - 1)
        def _():
            send_wo().wait()
            for i in range(items // tile):
                send_hidden(i).wait()

    def rows(cols):
        return pl.BlockSpec((tile, cols), lambda t: (t, 0))

    return pl.pallas_call(
        kernel,
        out_shape=[
            pltpu.HBM((items, hid), BF),
            jax.ShapeDtypeStruct((items, hid), F32),
            pltpu.HBM((ny, width, hid), BF),
        ] + [jax.ShapeDtypeStruct((items, width), F32)] * ny,
        grid=(items // tile,),
        in_specs=[SMEM] + [rows(depth)] * ny + [VMEM] * (2 * many),
        out_specs=[HBM, rows(hid), HBM] + [rows(width)] * ny,
        scratch_shapes=[
            pltpu.VMEM((ny, hz, nx, in_rows, hid), BF),
            pltpu.VMEM((ny, hz, nx, out_rows, hid), F32),
            pltpu.VMEM((ny, width, hid), BF),
            pltpu.VMEM((items // tile, tile, hid), BF),
            pltpu.SemaphoreType.DMA,
            pltpu.SemaphoreType.DMA((items // tile,)),
        ],
        cost_estimate=pl.CostEstimate(
            flops=2 * items * hid * ny * (depth + width), bytes_accessed=12 << 20, transcendentals=items * hid),
        compiler_params=pltpu.CompilerParams(vmem_limit_bytes=48 << 20),
        name="encode",
    )(place, *feats, *near, *other)


def ask(codes, w_in, w_out, nz, nx, ns, rows_own, cap):
    levels, items = codes.shape
    in_rows, hid = w_in.shape
    out_rows = w_out.shape[0]
    owners = ns * nz * nx
    slots = owners * cap
    group = slots // nz
    digit_rows = 8
    lane = 128

    def kernel(codes_ref, wi_ref, wo_ref, slot_ref, pay_ref, col_ref, found_ref):
        fill = jnp.zeros((8 - levels, lane), I32)
        for t in range(items // lane):
            block = jnp.concatenate([codes_ref[:, t * lane:(t + 1) * lane], fill], axis=0).T
            for l in range(levels):
                col_ref[l, t * lane:(t + 1) * lane, :] = block[:, l:l + 1]
        found_ref[...] = jnp.zeros_like(found_ref)

        def level(l, carry):
            code_row, code_col = codes_ref[pl.ds(l, 1), :], col_ref[l]
            own_row, _ = split(code_row, rows_own)
            own_col, row_col = split(code_col, rows_own)
            first = lax.broadcasted_iota(I32, (items, items), 0)
            second = lax.broadcasted_iota(I32, (items, items), 1)
            before = jnp.where(second < first, jnp.where(own_col == own_row, 1.0, 0.0), 0.0)
            rank = jnp.sum(before, axis=1, keepdims=True).astype(I32)
            slot_ref[l] = own_col * cap + rank
            section, rest = split(own_col, nz * nx)
            spot = (rest * ns + section) * cap + rank
            value = (row_col + 1).astype(F32)
            lanes = lax.broadcasted_iota(I32, (items, slots), 1)
            want = jnp.sum(jnp.where(lanes == spot, value, 0.0), axis=0, keepdims=True).astype(I32)
            high, low = split(want, 32)
            found_ref[pl.ds(2 * l, 1), :] = high.astype(F32)
            found_ref[pl.ds(2 * l + 1, 1), :] = low.astype(F32)
            return carry

        lax.fori_loop(0, levels, level, 0)
        rest = jnp.zeros((digit_rows, hid - group), F32)
        for z in range(nz):
            pay_ref[z, :in_rows] = wi_ref[...]
            digits = jnp.concatenate([found_ref[:, z * group:(z + 1) * group], rest], axis=1)
            pay_ref[z, in_rows:] = jnp.concatenate([wo_ref[...].astype(F32), digits], axis=0).astype(BF)

    return pl.pallas_call(
        kernel,
        out_shape=[
            jax.ShapeDtypeStruct((levels, items, 1), I32),
            jax.ShapeDtypeStruct((nz, in_rows + out_rows + digit_rows, hid), BF),
        ],
        in_specs=[VMEM] * 3,
        out_specs=[VMEM] * 2,
        scratch_shapes=[pltpu.VMEM((levels, items, 1), I32), pltpu.VMEM((digit_rows, slots), F32)],
        name="ask",
    )(codes, w_in, w_out)


def pick(asked, book, owners):
    levels, lines, lane = asked.shape
    rows_own, width = book.shape[1:]
    slots = lines * lane
    cap = slots // owners
    tile = 256

    def kernel(asked_ref, book_ref, out_ref, col_ref):
        turned = asked_ref[0].T
        for t in range(lines):
            col_ref[t * lane:(t + 1) * lane, :] = turned[:, t:t + 1]

        def step(t, carry):
            col = col_ref[pl.ds(pl.multiple_of(t * tile, tile), tile), :]
            hit = jnp.where(lax.broadcasted_iota(I32, (tile, rows_own), 1) == col, 1.0, 0.0).astype(BF)
            got = mm(hit, book_ref[0]).astype(BF)
            out_ref[pl.ds(t * (tile // cap), tile // cap)] = got.reshape(tile // cap, cap, width)
            return carry

        lax.fori_loop(0, slots // tile, step, 0)

    return pl.pallas_call(
        kernel,
        out_shape=jax.ShapeDtypeStruct((owners, levels * cap, width), BF),
        grid=(levels,),
        in_specs=[
            pl.BlockSpec((1, lines, lane), lambda l: (l, 0, 0)),
            pl.BlockSpec((1, rows_own, width), lambda l: (l, 0, 0)),
        ],
        out_specs=pl.BlockSpec((owners, cap, width), lambda l: (0, l, 0)),
        scratch_shapes=[pltpu.VMEM((slots, 1), I32)],
        name="pick",
    )(asked, book)


def collect(asked, incoming, rows_own):
    levels, lines, lane = asked.shape
    owners, _, width = incoming.shape
    slots = lines * lane
    cap = slots // owners
    tile = 256

    def kernel(asked_ref, in_ref, out_ref):
        line = jnp.concatenate([asked_ref[0, t:t + 1, :] for t in range(lines)], axis=1)
        values = in_ref[...].reshape(slots, width)

        def step(t, carry):
            rows = lax.broadcasted_iota(I32, (tile, slots), 0) + t * tile
            hit = jnp.where(rows == line, 1.0, 0.0).astype(BF)
            out_ref[0, pl.ds(pl.multiple_of(t * tile, tile), tile), :] = mm(hit, values)
            return carry

        lax.fori_loop(0, rows_own // tile, step, 0)

    return pl.pallas_call(
        kernel,
        out_shape=jax.ShapeDtypeStruct((levels, rows_own, width), F32),
        grid=(levels,),
        in_specs=[
            pl.BlockSpec((1, lines, lane), lambda l: (l, 0, 0)),
            pl.BlockSpec((owners, cap, width), lambda l: (0, l, 0)),
        ],
        out_specs=pl.BlockSpec((1, rows_own, width), lambda l: (l, 0, 0)),
        compiler_params=pltpu.CompilerParams(vmem_limit_bytes=12 << 20),
        name="collect",
    )(asked, incoming)


def turn(feats, place):
    items, depth = feats[0].shape
    ny = len(feats)
    hy = ny // 2
    cols = 256

    def kernel(place_ref, *refs):
        here_ref, there_ref = refs[ny:]
        for k in range(ny):
            spot = place_ref[k]
            flat = refs[k][...].T

            @pl.when(spot < hy)
            def _():
                here_ref[spot] = flat

            @pl.when(spot >= hy)
            def _():
                there_ref[spot - hy] = flat

    out = pl.BlockSpec((hy, cols, items), lambda i: (0, i, 0))
    return pl.pallas_call(
        kernel,
        out_shape=[jax.ShapeDtypeStruct((hy, depth, items), BF)] * 2,
        grid=(depth // cols,),
        in_specs=[SMEM] + [pl.BlockSpec((items, cols), lambda i: (0, i))] * ny,
        out_specs=[out] * 2,
        cost_estimate=pl.CostEstimate(flops=0, bytes_accessed=8 << 20, transcendentals=0),
        name="turn",
    )(place, *feats)


def back(grads, hidden, slope, w_out, feats_there, place, step):
    items, hid = hidden.shape
    ny, width = w_out.shape[:2]
    hy = ny // 2
    rows = feats_there.shape[0]
    tile = rows // 4

    def kernel(place_ref, *refs):
        g_refs, refs = refs[:ny], refs[ny:]
        hid_ref, slope_ref, wo_ref, f_ref, pre_ref, here_ref, away_ref, there_ref = refs

        @pl.when(pl.program_id(0) == 0)
        def _():
            grads_all = jnp.concatenate([g_refs[k][...] for k in range(ny)], axis=1)
            w_all = jnp.concatenate([wo_ref[place_ref[k]] for k in range(ny)], axis=0)
            pre_ref[...] = (mm(grads_all, w_all) * slope_ref[...]).astype(BF)
            outs = mm(grads_all, hid_ref[...], ((0,), (0,)))
            for k in range(ny):
                spot = place_ref[k]
                block = outs[k * width:(k + 1) * width]

                @pl.when(spot < hy)
                def _():
                    here_ref[spot] = block

                @pl.when(spot >= hy)
                def _():
                    away_ref[spot - hy] = block.astype(BF)

        there_ref[...] = mm(f_ref[...], pre_ref[:, :step]).astype(BF)

    def whole(*shape):
        return pl.BlockSpec(shape, lambda t: (0,) * len(shape))

    return pl.pallas_call(
        kernel,
        out_shape=[
            jax.ShapeDtypeStruct((items, hid), BF),
            jax.ShapeDtypeStruct((hy, width, hid), F32),
            pltpu.HBM((hy, width, hid), BF),
            jax.ShapeDtypeStruct((rows, step), BF),
        ],
        grid=(rows // tile,),
        in_specs=[SMEM] + [VMEM] * (ny + 3) + [pl.BlockSpec((tile, items), lambda t: (t, 0))],
        out_specs=[
            whole(items, hid), whole(hy, width, hid), whole(hy, width, hid),
            pl.BlockSpec((tile, step), lambda t: (t, 0)),
        ],
        cost_estimate=pl.CostEstimate(flops=6 * items * hid * ny * width, bytes_accessed=6 << 20, transcendentals=0),
        name="back",
    )(place, *grads, hidden, slope, w_out, feats_there)


def cut_by_x(feats_t, pre, came, out_mine, out_came, order, nz, nx, c):
    items = feats_t.shape[2]
    hid = came.shape[1]
    in_rows = came.shape[0] // (nz * nx)
    hy = feats_t.shape[0]
    width = out_mine.shape[1]
    out_rows = hy * width // (nz * nx)
    both = in_rows + out_rows
    feats_t = feats_t.reshape(-1, items)
    out_mine = out_mine.reshape(hy * width, -1)
    out_came = out_came.reshape(hy * width, -1)
    group = 4
    many, few = group * nx * in_rows, group * nx * out_rows

    def kernel(order_ref, f_ref, p_ref, came_ref, om_ref, oc_ref, own_ref, *rest):
        sends, part = rest[:-1], rest[-1]
        total = (mm(f_ref[...], p_ref[...]) + came_ref[...].astype(F32)).reshape(group, nx, in_rows, hid)
        outs = (om_ref[...] + oc_ref[...].astype(F32)).reshape(group, nx, out_rows, hid)
        for g in range(group):
            part[:, :in_rows] = total[g]
            part[:, in_rows:] = outs[g]
            own_ref[g] = part[order_ref[0]]
            for k, send in enumerate(sends):
                send[g] = part[order_ref[k + 1]].astype(BF)

    block = pl.BlockSpec((group, both, hid), lambda t: (t, 0, 0))
    return pl.pallas_call(
        kernel,
        out_shape=[jax.ShapeDtypeStruct((nz, both, hid), F32)]
        + [jax.ShapeDtypeStruct((nz, both, hid), BF)] * (nx - 1),
        grid=(nz // group,),
        in_specs=[
            SMEM,
            pl.BlockSpec((many, items), lambda t: (t, 0)),
            pl.BlockSpec((items, hid), lambda t: (0, c)),
            pl.BlockSpec((many, hid), lambda t: (t, 0)),
            pl.BlockSpec((few, hid), lambda t: (t, c)),
            pl.BlockSpec((few, hid), lambda t: (t, c)),
        ],
        out_specs=[block] * nx,
        scratch_shapes=[pltpu.VMEM((nx, both, hid), F32)],
        cost_estimate=pl.CostEstimate(
            flops=2 * nz * nx * in_rows * items * hid, bytes_accessed=8 << 20, transcendentals=0),
        compiler_params=pltpu.CompilerParams(vmem_limit_bytes=16 << 20),
        name="cut_by_x",
    )(order, feats_t, pre, came, out_mine, out_came)


def shards(features, w_in, w_out, codebook, codes, decoder_grad):
    s, x, y = lax.axis_index("s"), lax.axis_index("x"), lax.axis_index("y")
    ns, nz, nx, ny = (lax.axis_size(a) for a in ("s", "z", "x", "y"))
    owners = ns * nz * nx
    items, depth = features.shape
    levels, rows_own, width = codebook.shape
    cap = 2 * items // owners
    slots = owners * cap
    hid = w_in.shape[1]
    in_rows, out_rows = w_in.shape[0], w_out.shape[0]
    items_all = items * owners
    hy = ny // ns

    slot_all, payload = ask(codes, w_in, w_out, nz, nx, ns, rows_own, cap)
    got_z = exchange(payload, "z")
    w_z, digits = got_z[:, :in_rows + out_rows], got_z[:, in_rows + out_rows:, :slots // nz]
    feats = [features, shift(features, "y", 1), shift(features, "y", 2), shift(features, "y", -1)]
    hz = nz // 2
    from_left, from_right = shift(w_z, "x", 1), shift(w_z, "x", -1)
    near = [w_z, from_left, from_right, shift(from_left[:hz], "x", 1), shift(from_right[hz:], "x", -1)]
    spans = [(0, 0, 2), (1, 0, 2), (3, 0, 2), (2, 0, 1), (2, 1, 2)]
    other = [shift(block, "s", 1) for block in near]
    steps = jnp.arange(ny, dtype=I32)
    x_place = (x - steps) % nx
    y_place = (y - steps - hy * s) % ny
    y_send = (y + steps - hy * s) % ny
    x_send = (x + steps) % nx

    slot_list = [slot_all[l, :, 0] for l in range(levels)]
    slot_ids = jnp.arange(slots)
    digit_by = [
        digits, shift(digits, "x", 1), shift(digits, "x", 2), shift(digits, "x", -1)]
    none = jnp.zeros_like(digits)
    by_x = jnp.stack([
        sum(jnp.where((x - k) % nx == xa, digit_by[k], none) for k in range(nx)) for xa in range(nx)])
    far_x = shift(by_x, "s", 1)
    by_sx = jnp.stack([jnp.where(s == sa, by_x, far_x) for sa in range(ns)])
    mine = ((x * ns + s) * cap + jnp.arange(cap))[None, :] == jnp.arange(slots // nz)[:, None]
    picked = mm(by_sx.reshape(-1, slots // nz), mine.astype(BF)).reshape(ns, nx, nz, -1, cap)
    picked = jnp.transpose(picked, (3, 0, 2, 1, 4)).reshape(-1, slots).astype(jnp.int32)
    asked = (picked[0::2] * 32 + picked[1::2] - 1)[:levels].reshape(levels, -1, 128)
    chosen = pick(asked, codebook, owners)
    rows_back = exchange(chosen, OWN)
    words = [
        mm(
            (slot_list[l][:, None] == slot_ids[None, :]).astype(BF),
            rows_back[:, l * cap:(l + 1) * cap].reshape(slots, width),
        )
        for l in range(levels)
    ]

    hidden, slope, w_out_all, *lat = encode(
        feats, near, other, spans, jnp.concatenate([x_place, y_place, y_send]), in_rows, out_rows
    )
    far = shift(lat[2], "y", 2)
    fwd = shift(lat[1], "y", 1)
    bwd = shift(lat[3], "y", -1)
    feats_here, feats_there = turn(feats, y_place)
    words = lax.optimization_barrier(words)
    latent = lat[0] + fwd + bwd + far

    residual = latent
    pull_sum = jnp.zeros_like(latent)
    outgoing = []
    for l in range(levels):
        placed = mm((slot_ids[:, None] == slot_list[l][None, :]).astype(BF), residual.astype(BF))
        outgoing.append(placed.astype(BF).reshape(owners, cap, width))
        residual = residual - words[l]
        pull_sum = pull_sum + residual
    latent_grad = (
        (decoder_grad.astype(F32) + 2.0 * BETA * pull_sum) / jnp.sqrt(F32(items_all))
    ).astype(BF)
    grads = [latent_grad, shift(latent_grad, "y", 1), shift(latent_grad, "y", 2), shift(latent_grad, "y", -1)]
    incoming = exchange(jnp.concatenate(outgoing, axis=1), OWN)
    code_sums = collect(asked, incoming, rows_own)

    pieces = 2
    step = hid // pieces
    there_rows = feats_there.reshape(hy * depth, items)
    pre_grad, out_here, out_away, there_first = back(grads, hidden, slope, w_out_all, there_rows, y_place, step)
    out_came = shift(out_away, "s", 1)
    in_list, out_list = [], []
    for c in range(pieces):
        there = there_first if c == 0 else mm(there_rows, pre_grad[:, c * step:(c + 1) * step]).astype(BF)
        came = shift(there, "s", 1)
        own, to_1, to_2, to_3 = cut_by_x(feats_here, pre_grad, came, out_here, out_came, x_send, nz, nx, c)
        sum_x = (
            own
            + shift(to_1, "x", 1).astype(F32)
            + shift(to_2, "x", 2).astype(F32)
            + shift(to_3, "x", -1).astype(F32)
        ).astype(BF)
        over_z = exchange(sum_x, "z")
        in_list.append(jnp.sum(over_z[:, :in_rows].astype(F32), axis=0))
        out_list.append(jnp.sum(over_z[:, in_rows:].astype(F32), axis=0))
    return (jnp.concatenate(in_list, axis=1), jnp.concatenate(out_list, axis=1), code_sums)


def solution(mesh):
    fine = Mesh(mesh.devices.reshape(2, 8, 4, 4), ("s", "z", "x", "y"))
    in_specs = (
        P(OWN, "y"),
        P(OWN, "y"),
        P(OWN, "y"),
        P(None, OWN, "y"),
        P(None, OWN),
        P(OWN, "y"),
    )
    out_specs = (P(OWN, "y"), P(OWN, "y"), P(None, OWN, "y"))
    return jax.shard_map(shards, mesh=fine, in_specs=in_specs, out_specs=out_specs, check_vma=False)
```
